32 devices in a mesh: blk: 32 (over z, y, x, core), col: 1.
Axes of the slice: x: 2, y: 2, z: 4, core: 2. Of those that a mesh axis runs over, the one named last changes fastest.
Arguments:
- kernel: float32 [2048, 1, 2048], P('blk', 'col'), may hold values from -8 to 60, as said below
- ritz_block: float32 [2048, 128], P(('blk', 'col')), may hold values from -0.125 to 0.125
- search_block: float32 [2048, 128], P(('blk', 'col')), may hold values from -0.125 to 0.125
- precond_diag: float32 [2048], P(('blk', 'col')), may hold values from 3 to 30
Outputs:
- new_ritz: float32 [2048, 128], P(('blk', 'col'))
- correction: float32 [2048, 128], P(('blk', 'col'))
- residual_norms: float32 [2, 128], replicated
The draws below stay inside these ranges and needn't reach their ends.
Inputs may be any that keep to these rules, and one draw needn't show every extreme that they name: kernel holds a symmetric matrix K as stated in the reference program, with a positive diagonal.
All inputs are finite; a program needn't handle non-finite values.
Results may differ from the reference program's by a relative error of at most 0.0003.
Values sent between devices are 32-bit elements; how exact they have to be, the bound alone decides.
No kernel may reach another device: no remote copies, remote signals or barrier semaphores. Data moves between devices by JAX's collectives and lax.ppermute only.
A program may use at most 64 MiB of HBM per device.

```python
import math
import jax
import jax.numpy as jnp
from jax import lax

ROWS_DEV = 64
V = 128
ITERS = 2
N = 2048
QUARTER = 64


def draw_kernel(key, part):
    first_key, second_key = jax.random.split(jax.random.fold_in(key, 7))
    noise = jax.random.normal(first_key, (N, N), jnp.float32)
    upper_scale = 10.0
    scales = jnp.exp(jax.random.uniform(second_key, (N,), jnp.float32, 0.0, jnp.log(upper_scale)))
    roots = jnp.sqrt(scales)
    symmetric = (noise + noise.T) * (1.0 / jnp.sqrt(2.0 * N)) + 3.0 * jnp.eye(N, dtype=jnp.float32)
    matrix = symmetric * (roots[:, None] * roots[None, :])
    groups = ROWS_DEV // QUARTER
    matrix = matrix.reshape(N, N // ROWS_DEV, groups, QUARTER).transpose(0, 2, 1, 3)
    return matrix.reshape(N, groups, N // groups)


def level_of(key, shape, cuts, low, high):
    def one(dim, blocks):
        draws = jax.random.uniform(jax.random.fold_in(jax.random.fold_in(key, 6), dim), (blocks,), jnp.float32, low / len(cuts), high / len(cuts))
        return jnp.repeat(jnp.exp(draws), shape[dim] // blocks).reshape((-1,) + (1,) * (len(shape) - dim - 1))

    factor_of = one(*cuts[0])
    for cut in cuts[1:]:
        factor_of = factor_of * one(*cut)
    return factor_of


def scatter_about(stream_key, shape, deviation, bound, cuts=(), held_as=jnp.bfloat16):
    array = jax.random.normal(stream_key, shape, jnp.float32) * deviation
    if len(cuts) > 0:
        array = level_of(stream_key, shape, cuts, -0.22, 0.18) * array
    return jnp.clip(array, min=-bound, max=bound).astype(held_as)


def setup_inputs(seed: int = 0) -> dict:
    key_list = jax.random.split(jax.random.key(seed), 5)
    return {
        "kernel": draw_kernel(jax.random.fold_in(key_list[4], 71), 0),
        "ritz_block": scatter_about(key_list[1], (N, V), N ** -0.5, 0.125, ((0, 32),), jnp.float32),
        "search_block": scatter_about(key_list[2], (N, V), N ** -0.5, 0.125, ((0, 32),), jnp.float32),
        "precond_diag": jnp.clip(jnp.exp(math.log(30.0) - 2.3025851 * jax.random.uniform(key_list[3], (N,), jnp.float32) ** level_of(key_list[3], (N,), ((0, 32),), -0.2, 0.2)), 3.0, 30.0),
    }


highest = lax.Precision.HIGHEST

def apply_kernel(kernel, vectors):
    groups = ROWS_DEV // QUARTER
    count = vectors.shape[1]
    layout = vectors.reshape(N // ROWS_DEV, groups, QUARTER, count).transpose(1, 0, 2, 3)
    layout = layout.reshape(groups, N // groups, count)
    return jnp.einsum('iqj,qjm->im', kernel, layout, precision=highest)

def inner(former, latter):
    return lax.dot_general(former.astype(jnp.float32), latter.astype(jnp.float32), (((0,), (0,)), ((), ())), precision=highest, preferred_element_type=jnp.float32)

def coefficients(blocks, width):
    ritz_ritz, ritz_search, search_search, ritz_image, ritz_wimage, search_wimage = blocks
    metric = jnp.concatenate([jnp.concatenate([ritz_ritz, ritz_search], 1), jnp.concatenate([ritz_search.T, search_search], 1)], 0)
    projected = jnp.concatenate([jnp.concatenate([ritz_image, ritz_wimage], 1), jnp.concatenate([ritz_wimage.T, search_wimage], 1)], 0)
    lower_metric = jnp.linalg.cholesky(metric)
    halfway = lax.linalg.triangular_solve(lower_metric, projected[:, :width], left_side=True, lower=True)
    powered = lax.linalg.triangular_solve(lower_metric, halfway, left_side=True, lower=True, transpose_a=True)
    hermite = jnp.dot(powered.T, jnp.dot(metric, powered, precision=highest), precision=highest)
    lower_hermite = jnp.linalg.cholesky(hermite)
    mixing = lax.linalg.triangular_solve(lower_hermite, powered, left_side=False, lower=True, transpose_a=True)
    ritz_values = jnp.dot(mixing.T, jnp.dot(projected, mixing, precision=highest), precision=highest)
    return (mixing, ritz_values)

def update(vectors, images, search, search_images, mixing, ritz_values, precond):
    width = vectors.shape[1]
    upper_part = mixing[:width]
    lower_part = mixing[width:]
    next_ritz = jnp.dot(vectors, upper_part, precision=highest) + jnp.dot(search, lower_part, precision=highest)
    next_image = jnp.dot(images, upper_part, precision=highest) + jnp.dot(search_images, lower_part, precision=highest)
    residual = next_image - jnp.dot(next_ritz, ritz_values, precision=highest)
    squares = lax.optimization_barrier(jnp.sum(residual * residual, axis=0))
    divisor = jnp.maximum(jnp.abs(precond[:, None] - jnp.diagonal(ritz_values)[None, :]), 1.0)
    return (next_ritz, next_image, residual / divisor, squares)

def reference(kernel, ritz_block, search_block, precond_diag):
    width = ritz_block.shape[1]
    vectors = ritz_block
    search = search_block
    images = apply_kernel(kernel, vectors)
    search_images = apply_kernel(kernel, search)
    norm_rows = []
    for iteration in range(ITERS):
        if iteration > 0:
            search_images = apply_kernel(kernel, search)
        blocks = (inner(vectors, vectors), inner(vectors, search), inner(search, search), inner(vectors, images), inner(vectors, search_images), inner(search, search_images))
        mixing, ritz_values = coefficients(blocks, width)
        vectors, images, search, squares = update(vectors, images, search, search_images, mixing, ritz_values, precond_diag)
        norm_rows.append(jnp.sqrt(squares))
    return (vectors, search, jnp.stack(norm_rows, 0))
```

```python
import jax
import jax.numpy as jnp
from jax import lax
from jax.experimental import pallas as pl
from jax.experimental.pallas import tpu as pltpu
from jax.sharding import PartitionSpec as P

ITERS = 2
F32 = jnp.float32
highest = lax.Precision.HIGHEST
CHUNK = 512


def params():
    return pltpu.CompilerParams(vmem_limit_bytes=56 << 20)


def mm(a, b, ca=1, cb=0):
    return lax.dot_general(
        a, b, (((ca,), (cb,)), ((), ())), precision=highest, preferred_element_type=F32
    )


def inverse_factor(matrix):
    n = matrix.shape[0]
    count = n // 8
    lane = lax.broadcasted_iota(jnp.int32, (8, n), 1)
    sub = lax.broadcasted_iota(jnp.int32, (8, n), 0)
    a = [matrix[8 * v : 8 * v + 8, :] for v in range(count)]

    def wide(x):
        return jnp.broadcast_to(x, (8, n))

    for k in range(0, n, 2):
        r, s = divmod(k, 8)
        row0 = wide(a[r][s : s + 1, :])
        row1 = wide(a[r][s + 1 : s + 2, :])
        p00 = wide(a[r][s : s + 1, k : k + 1])
        p01 = wide(a[r][s : s + 1, k + 1 : k + 2])
        p11 = wide(a[r][s + 1 : s + 2, k + 1 : k + 2])
        scale = 1.0 / (p00 * p11 - p01 * p01)
        q00 = p11 * scale
        q01 = -p01 * scale
        q11 = p00 * scale
        at0 = lane == k
        at1 = lane == k + 1
        g0 = jnp.where(at0, q00, jnp.where(at1, q01, q00 * row0 + q01 * row1))
        g1 = jnp.where(at0, q01, jnp.where(at1, q11, q01 * row0 + q11 * row1))
        inside = at0 | at1
        for v in range(r, count):
            if v == r and s == 6:
                continue
            c0 = wide(a[v][:, k : k + 1])
            c1 = wide(a[v][:, k + 1 : k + 2])
            new = jnp.where(inside, 0.0, a[v]) - c0 * g0 - c1 * g1
            a[v] = jnp.where(sub > s + 1, new, a[v]) if v == r else new
    even = (sub % 2) == 0
    rows = []
    for v in range(count):
        here = sub + 8 * v
        across = jnp.where(even, here + 1, here - 1)
        diag = wide(jnp.sum(jnp.where(lane == here, a[v], 0.0), axis=1, keepdims=True))
        off = wide(jnp.sum(jnp.where(lane == across, a[v], 0.0), axis=1, keepdims=True))
        left = jnp.where(lane < (sub // 2) * 2 + 8 * v, a[v], 0.0)
        unit = jnp.where(lane == here, 1.0, left)
        above = pltpu.roll(unit, 1, 0)
        ratio = off / pltpu.roll(diag, 1, 0)
        norm = lax.rsqrt(jnp.where(even, diag, diag - off * ratio))
        rows.append(jnp.where(even, unit, unit - ratio * above) * norm)
    return jnp.concatenate(rows, 0)


def device_of(me, dz, k, dc, rings):
    z = lax.rem(me // 8 + (dz + rings), rings)
    low = lax.rem(me, 8)
    return z * 8 + jnp.bitwise_xor(low, 2 * k + dc)


def layout_of(rings):
    half = rings // 2
    out = []
    for dc in (0, 1):
        out += [(0, (0, 1), dc), (0, (2, 3), dc)]
        for t in range(1, half):
            out += [(-t, (0, 1), dc), (-t, (2, 3), dc), (t, (0, 1), dc), (t, (2, 3), dc)]
        out += [(-half, (0, 1), dc), (half, (2, 3), dc)]
    return out


def gather(block, n):
    rings = n // 8
    half = rings // 2

    def swap(x, m):
        return lax.ppermute(x, "blk", [(i, i ^ m) for i in range(n)])

    def turn(x, d):
        return lax.ppermute(x, "blk", [(i, ((i // 8 + d) % rings) * 8 + i % 8) for i in range(n)])

    by_x, by_y, by_xy = swap(block, 2), swap(block, 4), swap(block, 6)
    first = jnp.concatenate([block, by_x], 0)
    second = jnp.concatenate([by_y, by_xy], 0)
    near = [first, second]
    up_a, up_b, down_a, down_b = first, second, first, second
    for t in range(1, half):
        up_a, down_b = turn(up_a, 1), turn(down_b, -1)
        up_b, down_a = turn(up_b, 1), turn(down_a, -1)
        near += [up_a, up_b, down_a, down_b]
    near += [turn(up_a, 1), turn(down_b, -1)]
    return near + [swap(x, 1) for x in near]


def assemble(me, pieces, rows, rings, place):
    for piece, (dz, ks, dc) in zip(pieces, layout_of(rings)):
        for slot, k in enumerate(ks):
            place(piece, slot, device_of(me, dz, k, dc, rings))


def first_product(rings, rows, me_ref, kernel_ref, *refs):
    pieces, (y_ref, ky_ref, diag_ref, table) = refs[:-4], refs[-4:]
    width = y_ref.shape[1] // 2
    step = 2 * rows + 8

    def place(piece, slot, device):
        base = slot * step
        at = pl.ds(pl.multiple_of(device * rows, rows), rows)
        y_ref[at, :width] = piece[base : base + rows, :]
        y_ref[at, width:] = piece[base + rows : base + 2 * rows, :]
        table[pl.ds(device, 1), :] = piece[base + 2 * rows : base + 2 * rows + 1, :]

    table[...] = jnp.zeros_like(table)
    assemble(me_ref[0], pieces, rows, rings, place)
    diag_ref[...] = table[...].T
    result = mm(kernel_ref[...], y_ref[...])
    ky_ref[:rows, :] = result[:, :width]
    ky_ref[rows:, :] = result[:, width:]


def metric_factor(y_ref, out_ref):
    total, double = y_ref.shape
    width = double // 2
    chunk = min(CHUNK, total)

    def add(i, acc):
        part = y_ref[pl.ds(pl.multiple_of(i * chunk, chunk), chunk), :]
        return acc + mm(part, part, 0, 0)

    metric = lax.fori_loop(0, total // chunk, add, jnp.zeros((double, double), F32))
    upper = inverse_factor(metric[:width, :width])
    cross = mm(upper, metric[:width, width:])
    lower = inverse_factor(metric[width:, width:] - mm(cross, cross, 0, 0))
    out_ref[:width, :width] = upper
    out_ref[:width, width:] = jnp.zeros((width, width), F32)
    out_ref[width:, :width] = -mm(lower, mm(cross, upper, 0, 0))
    out_ref[width:, width:] = lower


def divided(residual, diag, values):
    eye = lax.broadcasted_iota(jnp.int32, values.shape, 0) == lax.broadcasted_iota(
        jnp.int32, values.shape, 1
    )
    level = jnp.sum(jnp.where(eye, values, 0.0), axis=0, keepdims=True)
    return residual / jnp.maximum(jnp.abs(diag - level), 1.0)


def first_step(y_ref, ky_ref, factor_ref, diag_ref, y2_ref, kx_ref, small_ref, norm_ref):
    total, double = y_ref.shape
    width = double // 2
    rows = diag_ref.shape[0]
    chunk = min(CHUNK, total)

    def add(i, acc):
        at = pl.ds(pl.multiple_of(i * chunk, chunk), chunk)
        return acc + mm(y_ref[at, :], ky_ref[at, :], 0, 0)

    g = lax.fori_loop(0, total // chunk, add, jnp.zeros((double, double), F32))
    factor = factor_ref[...]
    head = g[:width, :]
    side = jnp.concatenate([g[:width, :width], g[:width, width:].T], 0)
    whole = jnp.concatenate(
        [head, jnp.concatenate([g[:width, width:].T, g[width:, width:]], 1)], 0
    )
    z = mm(factor, side)
    small = inverse_factor(mm(z, z, 0, 0))
    mixing = mm(factor, mm(z, small, 1, 1), 0, 0)
    values = mm(mixing, mm(whole, mixing), 0, 0)
    both = jnp.concatenate([mixing, mm(mixing, values)], 1)
    small_ref[...] = values

    def update(i, acc):
        at = pl.ds(pl.multiple_of(i * chunk, chunk), chunk)
        pair = mm(y_ref[at, :], both)
        image = mm(ky_ref[at, :], mixing)
        y2_ref[at, :width] = pair[:, :width]
        kx_ref[at, :] = image
        residual = image - pair[:, width:]
        y2_ref[at, width:] = residual
        return acc + jnp.sum(residual * residual, axis=0, keepdims=True)

    squares = lax.fori_loop(0, total // chunk, update, jnp.zeros((1, width), F32))
    norm_ref[...] = jnp.sqrt(squares)
    for b in range(total // rows):
        at = pl.ds(b * rows, rows)
        y2_ref[at, width:] = divided(y2_ref[at, width:], diag_ref[:rows, b : b + 1], values)


def with_product(rings, rows, me_ref, kernel_ref, y_ref, factor_ref, diag_ref, *refs):
    pieces = refs[:-6]
    y2_ref, kx_ref, small_ref, norm_ref, kw_ref, ky_ref = refs[-6:]
    width = kx_ref.shape[1]

    def place(piece, slot, device):
        base = slot * 2 * rows
        at = pl.ds(pl.multiple_of(device * rows, rows), rows)
        ky_ref[at, :width] = piece[base : base + rows, :]
        ky_ref[at, width:] = piece[base + rows : base + 2 * rows, :]

    assemble(me_ref[0], pieces, rows, rings, place)
    first_step(
        y_ref, ky_ref, factor_ref, diag_ref.at[:rows, :], y2_ref, kx_ref, small_ref, norm_ref
    )
    kw_ref[...] = mm(kernel_ref[...], y2_ref[:, width:])


def second_factor(y2_ref, gram_ref, factor_ref):
    total, double = y2_ref.shape
    width = double // 2
    chunk = min(CHUNK, total)

    def add(i, acc):
        at = pl.ds(pl.multiple_of(i * chunk, chunk), chunk)
        return acc + mm(y2_ref[at, :], y2_ref[at, width:], 0, 0)

    gram = lax.fori_loop(0, total // chunk, add, jnp.zeros((double, width), F32))
    cross = gram[:width]
    gram_ref[...] = cross
    factor_ref[...] = inverse_factor(gram[width:] - mm(cross, cross, 0, 0))


def second_step(
    y2_ref, image_ref, small_ref, cross_ref, factor_ref, own_y2, own_image, own_diag, outs
):
    ritz_ref, search_ref, norm_ref = outs
    total, double = y2_ref.shape
    width = double // 2
    chunk = min(CHUNK, total)

    def add(i, acc):
        at = pl.ds(pl.multiple_of(i * chunk, chunk), chunk)
        return acc + mm(y2_ref[at, :], image_ref[at, width:], 0, 0)

    g = lax.fori_loop(0, total // chunk, add, jnp.zeros((double, width), F32))
    values, cross, factor = small_ref[...], cross_ref[...], factor_ref[...]
    f_t = g[:width].T
    z = mm(factor, f_t - mm(cross, values, 0, 0))
    small = inverse_factor(mm(values, values, 0, 0) + mm(z, z, 0, 0))
    lower = mm(factor, mm(z, small, 1, 1), 0, 0)
    upper = mm(values, small, 1, 1) - mm(cross, lower)
    mixing = jnp.concatenate([upper, lower], 0)
    whole = jnp.concatenate(
        [jnp.concatenate([values, g[:width]], 1), jnp.concatenate([f_t, g[width:]], 1)], 0
    )
    values2 = mm(mixing, mm(whole, mixing), 0, 0)
    turned = mm(mixing, values2)

    def update(i, acc):
        at = pl.ds(pl.multiple_of(i * chunk, chunk), chunk)
        residual = mm(image_ref[at, :], mixing) - mm(y2_ref[at, :], turned)
        return acc + jnp.sum(residual * residual, axis=0, keepdims=True)

    squares = lax.fori_loop(0, total // chunk, update, jnp.zeros((1, width), F32))
    norm_ref[...] = jnp.sqrt(squares)
    own = own_y2()
    ritz = mm(own, mixing)
    ritz_ref[...] = ritz
    residual = mm(own_image(), mixing) - mm(ritz, values2)
    search_ref[...] = divided(residual, own_diag(), values2)


def last_step(rings, rows, me_ref, y2_ref, kx_ref, small_ref, cross_ref, factor_ref, own_ref, *refs):
    pieces = refs[:-4]
    ritz_ref, search_ref, norm_ref, image_ref = refs[-4:]
    width = kx_ref.shape[1]
    me = me_ref[0]

    def place(piece, slot, device):
        at = pl.ds(pl.multiple_of(device * rows, rows), rows)
        image_ref[at, width:] = piece[slot * rows : (slot + 1) * rows, :]

    assemble(me, pieces, rows, rings, place)
    image_ref[:, :width] = kx_ref[...]
    mine = pl.ds(pl.multiple_of(me * rows, rows), rows)
    second_step(
        y2_ref,
        image_ref,
        small_ref,
        cross_ref,
        factor_ref,
        lambda: y2_ref[mine, :],
        lambda: image_ref[mine, :],
        lambda: own_ref[...],
        (ritz_ref, search_ref, norm_ref),
    )


def general_last(y2_ref, image_ref, small_ref, cross_ref, factor_ref, own_y2, own_image, own_diag, *outs):
    second_step(
        y2_ref,
        image_ref,
        small_ref,
        cross_ref,
        factor_ref,
        lambda: own_y2[...],
        lambda: own_image[...],
        lambda: own_diag[...],
        outs,
    )


def shape(*dims):
    return jax.ShapeDtypeStruct(dims, F32)


VMEM = pl.BlockSpec(memory_space=pltpu.VMEM)
SMEM = pl.BlockSpec(memory_space=pltpu.SMEM)


def ringed(n, kernel, ritz, search, diag):
    rows, width = ritz.shape
    rings = n // 8
    total = n * rows
    me = lax.axis_index("blk").astype(jnp.int32).reshape(1)
    lanes = max(128, -(-rows // 128) * 128)
    extra = jnp.zeros((8, width), F32).at[0, :rows].set(diag)
    sent = gather(jnp.concatenate([ritz, search, extra], 0), n)
    y, ky_own, diag_table = pl.pallas_call(
        lambda *refs: first_product(rings, rows, *refs),
        out_shape=(shape(total, 2 * width), shape(2 * rows, width), shape(width, max(n, 128))),
        in_specs=[SMEM, VMEM] + [VMEM] * len(sent),
        out_specs=(VMEM, VMEM, VMEM),
        scratch_shapes=[pltpu.VMEM((max(n, 128), width), F32)],
        compiler_params=params(),
        name="first_product",
    )(me, kernel, *sent)
    images = gather(ky_own, n)
    factor = pl.pallas_call(
        metric_factor,
        out_shape=shape(2 * width, 2 * width),
        in_specs=[VMEM],
        out_specs=VMEM,
        compiler_params=params(),
        name="metric_factor",
    )(y)
    y2, kx, values, norm1, kw_own = pl.pallas_call(
        lambda *refs: with_product(rings, rows, *refs),
        out_shape=(
            shape(total, 2 * width),
            shape(total, width),
            shape(width, width),
            shape(1, width),
            shape(rows, width),
        ),
        in_specs=[SMEM] + [VMEM] * (4 + len(images)),
        out_specs=(VMEM,) * 5,
        scratch_shapes=[pltpu.VMEM((total, 2 * width), F32)],
        compiler_params=params(),
        name="first_step",
    )(me, kernel, y, factor, diag_table, *images)
    images2 = gather(kw_own, n)
    cross, factor2 = pl.pallas_call(
        second_factor,
        out_shape=(shape(width, width), shape(width, width)),
        in_specs=[VMEM],
        out_specs=(VMEM, VMEM),
        compiler_params=params(),
        name="second_factor",
    )(y2)
    new_ritz, correction, norm2 = pl.pallas_call(
        lambda *refs: last_step(rings, rows, *refs),
        out_shape=(shape(rows, width), shape(rows, width), shape(1, width)),
        in_specs=[SMEM] + [VMEM] * (6 + len(images2)),
        out_specs=(VMEM,) * 3,
        scratch_shapes=[pltpu.VMEM((total, 2 * width), F32)],
        compiler_params=params(),
        name="last_step",
    )(me, y2, kx, values, cross, factor2, diag[:, None], *images2)
    return new_ritz, correction, jnp.concatenate([norm1, norm2], 0)


def general(n, cols, kernel, ritz, search, diag):
    rows, width = ritz.shape
    axes = ("blk", "col")
    total = n * cols * rows
    q = lax.axis_index("col")

    def product(part):
        whole = lax.psum_scatter(mm(kernel, part), "col", scatter_dimension=0, tiled=True)
        return whole

    own = jnp.concatenate([ritz, search], 1)
    part = lax.all_gather(own, "blk", axis=0, tiled=True)
    y = lax.all_gather(own, axes, axis=0, tiled=True)
    ky = lax.all_gather(product(part), axes, axis=0, tiled=True)
    table = lax.all_gather(diag, axes, axis=0, tiled=True).reshape(n * cols, rows).T
    factor = pl.pallas_call(
        metric_factor,
        out_shape=shape(2 * width, 2 * width),
        in_specs=[VMEM],
        out_specs=VMEM,
        compiler_params=params(),
        name="metric_factor",
    )(y)
    y2, kx, values, norm1 = pl.pallas_call(
        first_step,
        out_shape=(shape(total, 2 * width), shape(total, width), shape(width, width), shape(1, width)),
        in_specs=[VMEM] * 4,
        out_specs=(VMEM,) * 4,
        compiler_params=params(),
        name="first_step",
    )(y, ky, factor, table)
    held = y2[:, width:].reshape(n, cols, rows, width)
    part2 = lax.dynamic_index_in_dim(held, q, 1, keepdims=False).reshape(n * rows, width)
    kw = lax.all_gather(product(part2), axes, axis=0, tiled=True)
    cross, factor2 = pl.pallas_call(
        second_factor,
        out_shape=(shape(width, width), shape(width, width)),
        in_specs=[VMEM],
        out_specs=(VMEM, VMEM),
        compiler_params=params(),
        name="second_factor",
    )(y2)
    image = jnp.concatenate([kx, kw], 1)
    at = (lax.axis_index("blk") * cols + q) * rows
    new_ritz, correction, norm2 = pl.pallas_call(
        general_last,
        out_shape=(shape(rows, width), shape(rows, width), shape(1, width)),
        in_specs=[VMEM] * 8,
        out_specs=(VMEM,) * 3,
        compiler_params=params(),
        name="last_step",
    )(
        y2,
        image,
        values,
        cross,
        factor2,
        lax.dynamic_slice_in_dim(y2, at, rows, 0),
        lax.dynamic_slice_in_dim(image, at, rows, 0),
        diag[:, None],
    )
    return new_ritz, correction, jnp.concatenate([norm1, norm2], 0)


def solution(mesh):
    n, cols = mesh.shape["blk"], mesh.shape["col"]
    placed = (
        P("blk", "col", None),
        P(("blk", "col"), None),
        P(("blk", "col"), None),
        P(("blk", "col")),
    )

    def per_device(kernel, ritz_block, search_block, precond_diag):
        rows = kernel[:, 0, :]
        if cols == 1 and n % 16 == 0 and ritz_block.shape[0] <= ritz_block.shape[1]:
            return ringed(n, rows, ritz_block, search_block, precond_diag)
        return general(n, cols, rows, ritz_block, search_block, precond_diag)

    return jax.shard_map(
        per_device,
        mesh=mesh,
        in_specs=placed,
        out_specs=(P(("blk", "col"), None), P(("blk", "col"), None), P()),
        check_vma=False,
    )
```

```python
import jax
import jax.numpy as jnp
from jax import lax
from jax.experimental import pallas as pl
from jax.experimental.pallas import tpu as pltpu
from jax.sharding import PartitionSpec as P

ITERS = 2
F32 = jnp.float32
BF16 = jnp.bfloat16
highest = lax.Precision.HIGHEST
CHUNK = 512


def params():
    return pltpu.CompilerParams(vmem_limit_bytes=56 << 20)


def mm(a, b, ca=1, cb=0):
    return lax.dot_general(
        a, b, (((ca,), (cb,)), ((), ())), precision=highest, preferred_element_type=F32
    )


def halves(x):
    top = x.astype(BF16)
    return top, (x - top.astype(F32)).astype(BF16)


def mm3(a, b, ca=1, cb=0):
    a1, a2 = halves(a)
    b1, b2 = halves(b)
    return lax.dot_general(
        jnp.concatenate([a1, a1, a2], ca),
        jnp.concatenate([b1, b2, b1], cb),
        (((ca,), (cb,)), ((), ())),
        preferred_element_type=F32,
    )


def total_of(xs, ys):
    out = xs[0] * ys[0]
    for x, y in zip(xs[1:], ys[1:]):
        out = out + x * y
    return out


def solved(entry, columns):
    size = len(columns[0])
    if size == 2:
        x, y, z = entry(0, 0), entry(0, 1), entry(1, 1)
        scale = 1.0 / (x * z - y * y)
        q00, q01, q11 = z * scale, -(y * scale), x * scale
        return [[q00 * c[0] + q01 * c[1], q01 * c[0] + q11 * c[1]] for c in columns]
    h = size // 2
    side = [[entry(i, h + j) for i in range(h)] for j in range(h)]
    done = solved(entry, side + [c[:h] for c in columns])
    ties, upper = done[:h], done[h:]
    rest = {
        (i, j): entry(h + i, h + j) - total_of(side[i], ties[j])
        for j in range(h)
        for i in range(j + 1)
    }
    lower = solved(
        lambda i, j: rest[i, j],
        [[c[h + j] - total_of(ties[j], c[:h]) for j in range(h)] for c in columns],
    )
    return [
        [u[i] - total_of([ties[j][i] for j in range(h)], g) for i in range(h)] + g
        for u, g in zip(upper, lower)
    ]


def inverse_factor(matrix, panel=32, step=8):
    n = matrix.shape[0]
    lane = lax.broadcasted_iota(jnp.int32, (8, n), 1)
    sub = lax.broadcasted_iota(jnp.int32, (8, n), 0)
    a = [matrix[8 * v : 8 * v + 8, :] for v in range(n // 8)]

    def along(x, j):
        return jnp.broadcast_to(x[:, j : j + 1], (8, n))

    def down(x, i):
        return jnp.broadcast_to(x[i : i + 1, :], (8, n))

    rows = []
    for first in range(0, n, panel):
        last = (first + panel) // 8
        multipliers = []
        for k in range(first, first + panel, step):
            r = k // 8
            own = [along(a[r], k + j) for j in range(step)]
            pivot = {(i, j): down(own[j], i) for j in range(step) for i in range(j + 1)}
            inside = (lane >= k) & (lane < k + step)
            right = [
                jnp.where(lane == k + i, 1.0, jnp.where(inside, 0.0, down(a[r], i)))
                for i in range(step)
            ]
            g = solved(lambda i, j: pivot[i, j], [right])[0]
            finished, factor, norms = [], {}, []
            for i in range(step):
                y, d = right[i], pivot[i, i]
                for j in range(i):
                    e = pivot[j, i]
                    for m in range(j):
                        e = e - factor[i, m] * factor[j, m]
                    factor[i, j] = e * norms[j]
                for j in range(i):
                    d = d - factor[i, j] * factor[i, j]
                    y = y - factor[i, j] * finished[j]
                norms.append(lax.rsqrt(d))
                finished.append(y * norms[i])
            row, held = finished[0], g[0]
            for i in range(1, step):
                row = jnp.where(sub == i, finished[i], row)
                held = jnp.where(sub == i, g[i], held)
            rows.append(jnp.where(lane <= sub + k, row, 0.0))
            multipliers.append(
                jnp.where((lane >= k + step) & (lane < first + panel), 0.0, held)
            )
            for v in range(r + 1, last):
                other = [along(a[v], k + j) for j in range(step)]
                a[v] = jnp.where(inside, 0.0, a[v]) - total_of(other, g)
        if last < n // 8:
            change = mm(
                jnp.concatenate(a[first // 8 : last], 0), jnp.concatenate(multipliers, 0), 0, 0
            )
            inside = (lane >= first) & (lane < first + panel)
            for v in range(last, n // 8):
                a[v] = jnp.where(inside, 0.0, a[v]) - change[8 * v : 8 * v + 8]
    return jnp.concatenate(rows, 0)


def device_of(me, dz, k, dc, rings):
    z = lax.rem(me // 8 + (dz + rings), rings)
    low = lax.rem(me, 8)
    return z * 8 + jnp.bitwise_xor(low, 2 * k + dc)


def layout_of(rings):
    half = rings // 2
    chips = [(0, (0, 1, 2, 3))]
    for t in range(1, half):
        chips += [(-t, (0, 1, 2, 3)), (t, (0, 1, 2, 3))]
    chips += [(-half, (0, 1)), (half, (2, 3))]
    return [chip + (dc,) for dc in (0, 1) for chip in chips]


def gather(block, n, tag):
    rings = n // 8
    half = rings // 2

    def send(x, pairs, name):
        with jax.named_scope(tag + name):
            return lax.ppermute(x, "blk", pairs)

    def swap(x, m, name):
        return send(x, [(i, i ^ m) for i in range(n)], name)

    def turn(x, d, name):
        pairs = [(i, ((i // 8 + d) % rings) * 8 + i % 8) for i in range(n)]
        return send(x, pairs, name)

    parts = [block, swap(block, 2, "_x"), swap(block, 4, "_y"), swap(block, 6, "_xy")]
    own = jnp.concatenate(parts, 0)
    near, up, down = [own], own, own
    for t in range(1, half):
        up, down = turn(up, 1, "_up"), turn(down, -1, "_down")
        near += [up, down]
    middle = own.shape[0] // 2
    near.append(turn(up[:middle], 1, "_lastup"))
    near.append(turn(down[middle:], -1, "_lastdown"))
    return near + [swap(x, 1, f"_core{i}") for i, x in enumerate(near)]


def assemble(me, pieces, rows, rings, place):
    for piece, (dz, ks, dc) in zip(pieces, layout_of(rings)):
        for slot, k in enumerate(ks):
            place(piece, slot, device_of(me, dz, k, dc, rings))


def first_product(rings, rows, me_ref, kernel_ref, *refs):
    pieces, (y_ref, ky_ref, diag_ref, table) = refs[:-4], refs[-4:]
    width = y_ref.shape[1] // 2
    step = 2 * rows + 8

    def place(piece, slot, device):
        base = slot * step
        at = pl.ds(pl.multiple_of(device * rows, rows), rows)
        y_ref[at, :width] = piece[base : base + rows, :]
        y_ref[at, width:] = piece[base + rows : base + 2 * rows, :]
        table[pl.ds(device, 1), :] = piece[base + 2 * rows : base + 2 * rows + 1, :]

    table[...] = jnp.zeros_like(table)
    assemble(me_ref[0], pieces, rows, rings, place)
    diag_ref[...] = table[...].T
    result = mm3(kernel_ref[...], y_ref[...])
    ky_ref[:rows, :] = result[:, :width]
    ky_ref[rows:, :] = result[:, width:]


def metric_head(y_ref, metric_ref, upper_ref):
    total, double = y_ref.shape
    width = double // 2
    chunk = min(CHUNK, total)

    def add(i, acc):
        part = y_ref[pl.ds(pl.multiple_of(i * chunk, chunk), chunk), :]
        return acc + mm3(part, part, 0, 0)

    metric = lax.fori_loop(0, total // chunk, add, jnp.zeros((double, double), F32))
    metric_ref[...] = metric
    upper_ref[...] = inverse_factor(metric[:width, :width])


def metric_tail(metric_ref, upper_ref, out_ref):
    width = upper_ref.shape[0]
    upper = upper_ref[...]
    cross = mm(upper, metric_ref[:width, width:])
    lower = inverse_factor(metric_ref[width:, width:] - mm(cross, cross, 0, 0))
    out_ref[:width, :width] = upper
    out_ref[:width, width:] = jnp.zeros((width, width), F32)
    out_ref[width:, :width] = -mm(lower, mm(cross, upper, 0, 0))
    out_ref[width:, width:] = lower


def divided(residual, diag, values):
    eye = lax.broadcasted_iota(jnp.int32, values.shape, 0) == lax.broadcasted_iota(
        jnp.int32, values.shape, 1
    )
    level = jnp.sum(jnp.where(eye, values, 0.0), axis=0, keepdims=True)
    return residual / jnp.maximum(jnp.abs(diag - level), 1.0)


def first_step(y_ref, ky_ref, factor_ref, diag_ref, y2_ref, kx_ref, small_ref, norm_ref):
    total, double = y_ref.shape
    width = double // 2
    rows = diag_ref.shape[0]
    chunk = min(CHUNK, total)

    def add(i, acc):
        at = pl.ds(pl.multiple_of(i * chunk, chunk), chunk)
        return acc + mm3(y_ref[at, :], ky_ref[at, :], 0, 0)

    g = lax.fori_loop(0, total // chunk, add, jnp.zeros((double, double), F32))
    factor = factor_ref[...]
    head = g[:width, :]
    side = jnp.concatenate([g[:width, :width], g[:width, width:].T], 0)
    whole = jnp.concatenate(
        [head, jnp.concatenate([g[:width, width:].T, g[width:, width:]], 1)], 0
    )
    z = mm(factor, side)
    small = inverse_factor(mm(z, z, 0, 0))
    mixing = mm(factor, mm(z, small, 1, 1), 0, 0)
    values = mm(mixing, mm(whole, mixing), 0, 0)
    both = jnp.concatenate([mixing, mm(mixing, values)], 1)
    small_ref[...] = values

    def update(i, acc):
        at = pl.ds(pl.multiple_of(i * chunk, chunk), chunk)
        pair = mm3(y_ref[at, :], both)
        image = mm3(ky_ref[at, :], mixing)
        y2_ref[at, :width] = pair[:, :width]
        kx_ref[at, :] = image
        residual = image - pair[:, width:]
        y2_ref[at, width:] = residual
        return acc + jnp.sum(residual * residual, axis=0, keepdims=True)

    squares = lax.fori_loop(0, total // chunk, update, jnp.zeros((1, width), F32))
    norm_ref[...] = jnp.sqrt(squares)
    for b in range(total // rows):
        at = pl.ds(b * rows, rows)
        y2_ref[at, width:] = divided(y2_ref[at, width:], diag_ref[:rows, b : b + 1], values)


def with_product(rings, rows, me_ref, kernel_ref, y_ref, factor_ref, diag_ref, *refs):
    pieces = refs[:-6]
    y2_ref, kx_ref, small_ref, norm_ref, kw_ref, ky_ref = refs[-6:]
    width = kx_ref.shape[1]

    def place(piece, slot, device):
        base = slot * 2 * rows
        at = pl.ds(pl.multiple_of(device * rows, rows), rows)
        ky_ref[at, :width] = piece[base : base + rows, :]
        ky_ref[at, width:] = piece[base + rows : base + 2 * rows, :]

    assemble(me_ref[0], pieces, rows, rings, place)
    first_step(
        y_ref, ky_ref, factor_ref, diag_ref.at[:rows, :], y2_ref, kx_ref, small_ref, norm_ref
    )
    kw_ref[...] = mm3(kernel_ref[...], y2_ref[:, width:])


def second_factor(y2_ref, gram_ref, factor_ref):
    total, double = y2_ref.shape
    width = double // 2
    chunk = min(CHUNK, total)

    def add(i, acc):
        at = pl.ds(pl.multiple_of(i * chunk, chunk), chunk)
        return acc + mm3(y2_ref[at, :], y2_ref[at, width:], 0, 0)

    gram = lax.fori_loop(0, total // chunk, add, jnp.zeros((double, width), F32))
    cross = gram[:width]
    gram_ref[...] = cross
    factor_ref[...] = inverse_factor(gram[width:] - mm(cross, cross, 0, 0))


def second_step(
    y2_ref, image_ref, small_ref, cross_ref, factor_ref, own_y2, own_image, own_diag, outs
):
    ritz_ref, search_ref, norm_ref = outs
    total, double = y2_ref.shape
    width = double // 2
    chunk = min(CHUNK, total)

    def add(i, acc):
        at = pl.ds(pl.multiple_of(i * chunk, chunk), chunk)
        return acc + mm3(y2_ref[at, :], image_ref[at, width:], 0, 0)

    g = lax.fori_loop(0, total // chunk, add, jnp.zeros((double, width), F32))
    values, cross, factor = small_ref[...], cross_ref[...], factor_ref[...]
    f_t = g[:width].T
    z = mm(factor, f_t - mm(cross, values, 0, 0))
    small = inverse_factor(mm(values, values, 0, 0) + mm(z, z, 0, 0))
    lower = mm(factor, mm(z, small, 1, 1), 0, 0)
    upper = mm(values, small, 1, 1) - mm(cross, lower)
    mixing = jnp.concatenate([upper, lower], 0)
    whole = jnp.concatenate(
        [jnp.concatenate([values, g[:width]], 1), jnp.concatenate([f_t, g[width:]], 1)], 0
    )
    values2 = mm(mixing, mm(whole, mixing), 0, 0)
    turned = mm(mixing, values2)

    def update(i, acc):
        at = pl.ds(pl.multiple_of(i * chunk, chunk), chunk)
        residual = mm3(image_ref[at, :], mixing) - mm3(y2_ref[at, :], turned)
        return acc + jnp.sum(residual * residual, axis=0, keepdims=True)

    squares = lax.fori_loop(0, total // chunk, update, jnp.zeros((1, width), F32))
    norm_ref[...] = jnp.sqrt(squares)
    own = own_y2()
    ritz = mm(own, mixing)
    ritz_ref[...] = ritz
    residual = mm(own_image(), mixing) - mm(ritz, values2)
    search_ref[...] = divided(residual, own_diag(), values2)


def last_step(rings, rows, me_ref, y2_ref, kx_ref, small_ref, cross_ref, factor_ref, own_ref, *refs):
    pieces = refs[:-4]
    ritz_ref, search_ref, norm_ref, image_ref = refs[-4:]
    width = kx_ref.shape[1]
    me = me_ref[0]

    def place(piece, slot, device):
        at = pl.ds(pl.multiple_of(device * rows, rows), rows)
        image_ref[at, width:] = piece[slot * rows : (slot + 1) * rows, :]

    assemble(me, pieces, rows, rings, place)
    image_ref[:, :width] = kx_ref[...]
    mine = pl.ds(pl.multiple_of(me * rows, rows), rows)
    second_step(
        y2_ref,
        image_ref,
        small_ref,
        cross_ref,
        factor_ref,
        lambda: y2_ref[mine, :],
        lambda: image_ref[mine, :],
        lambda: own_ref[...],
        (ritz_ref, search_ref, norm_ref),
    )


def general_last(y2_ref, image_ref, small_ref, cross_ref, factor_ref, own_y2, own_image, own_diag, *outs):
    second_step(
        y2_ref,
        image_ref,
        small_ref,
        cross_ref,
        factor_ref,
        lambda: own_y2[...],
        lambda: own_image[...],
        lambda: own_diag[...],
        outs,
    )


def cost(us):
    return pl.CostEstimate(flops=int(us * 1e9), bytes_accessed=0, transcendentals=0)


def shape(*dims):
    return jax.ShapeDtypeStruct(dims, F32)


VMEM = pl.BlockSpec(memory_space=pltpu.VMEM)
SMEM = pl.BlockSpec(memory_space=pltpu.SMEM)


def metric_factor(y):
    width = y.shape[1] // 2
    with jax.named_scope("metric_head"):
        metric, upper = pl.pallas_call(
            metric_head,
            out_shape=(shape(2 * width, 2 * width), shape(width, width)),
            in_specs=[VMEM],
            out_specs=(VMEM, VMEM),
            compiler_params=params(),
            cost_estimate=cost(7),
            name="metric_head",
        )(y)
    with jax.named_scope("metric_tail"):
        return pl.pallas_call(
            metric_tail,
            out_shape=shape(2 * width, 2 * width),
            in_specs=[VMEM, VMEM],
            out_specs=VMEM,
            compiler_params=params(),
            cost_estimate=cost(7),
            name="metric_tail",
        )(metric, upper)


def ringed(n, kernel, ritz, search, diag):
    rows, width = ritz.shape
    rings = n // 8
    total = n * rows
    me = lax.axis_index("blk").astype(jnp.int32).reshape(1)
    lanes = max(128, -(-rows // 128) * 128)
    extra = jnp.zeros((8, width), F32).at[0, :rows].set(diag)
    sent = gather(jnp.concatenate([ritz, search, extra], 0), n, "ag1")
    y, ky_own, diag_table = pl.pallas_call(
        lambda *refs: first_product(rings, rows, *refs),
        out_shape=(shape(total, 2 * width), shape(2 * rows, width), shape(width, max(n, 128))),
        in_specs=[SMEM, VMEM] + [VMEM] * len(sent),
        out_specs=(VMEM, VMEM, VMEM),
        scratch_shapes=[pltpu.VMEM((max(n, 128), width), F32)],
        compiler_params=params(),
        name="first_product",
    )(me, kernel, *sent)
    images = gather(ky_own, n, "ag2")
    factor = metric_factor(y)
    y2, kx, values, norm1, kw_own = pl.pallas_call(
        lambda *refs: with_product(rings, rows, *refs),
        out_shape=(
            shape(total, 2 * width),
            shape(total, width),
            shape(width, width),
            shape(1, width),
            shape(rows, width),
        ),
        in_specs=[SMEM] + [VMEM] * (4 + len(images)),
        out_specs=(VMEM,) * 5,
        scratch_shapes=[pltpu.VMEM((total, 2 * width), F32)],
        compiler_params=params(),
        name="first_step",
    )(me, kernel, y, factor, diag_table, *images)
    images2 = gather(kw_own, n, "ag3")
    cross, factor2 = pl.pallas_call(
        second_factor,
        out_shape=(shape(width, width), shape(width, width)),
        in_specs=[VMEM],
        out_specs=(VMEM, VMEM),
        compiler_params=params(),
        name="second_factor",
    )(y2)
    new_ritz, correction, norm2 = pl.pallas_call(
        lambda *refs: last_step(rings, rows, *refs),
        out_shape=(shape(rows, width), shape(rows, width), shape(1, width)),
        in_specs=[SMEM] + [VMEM] * (6 + len(images2)),
        out_specs=(VMEM,) * 3,
        scratch_shapes=[pltpu.VMEM((total, 2 * width), F32)],
        compiler_params=params(),
        name="last_step",
    )(me, y2, kx, values, cross, factor2, diag[:, None], *images2)
    return new_ritz, correction, jnp.concatenate([norm1, norm2], 0)


def general(n, cols, kernel, ritz, search, diag):
    rows, width = ritz.shape
    axes = ("blk", "col")
    total = n * cols * rows
    q = lax.axis_index("col")

    def product(part):
        whole = lax.psum_scatter(mm(kernel, part), "col", scatter_dimension=0, tiled=True)
        return whole

    own = jnp.concatenate([ritz, search], 1)
    part = lax.all_gather(own, "blk", axis=0, tiled=True)
    y = lax.all_gather(own, axes, axis=0, tiled=True)
    ky = lax.all_gather(product(part), axes, axis=0, tiled=True)
    table = lax.all_gather(diag, axes, axis=0, tiled=True).reshape(n * cols, rows).T
    factor = metric_factor(y)
    y2, kx, values, norm1 = pl.pallas_call(
        first_step,
        out_shape=(shape(total, 2 * width), shape(total, width), shape(width, width), shape(1, width)),
        in_specs=[VMEM] * 4,
        out_specs=(VMEM,) * 4,
        compiler_params=params(),
        name="first_step",
    )(y, ky, factor, table)
    held = y2[:, width:].reshape(n, cols, rows, width)
    part2 = lax.dynamic_index_in_dim(held, q, 1, keepdims=False).reshape(n * rows, width)
    kw = lax.all_gather(product(part2), axes, axis=0, tiled=True)
    cross, factor2 = pl.pallas_call(
        second_factor,
        out_shape=(shape(width, width), shape(width, width)),
        in_specs=[VMEM],
        out_specs=(VMEM, VMEM),
        compiler_params=params(),
        name="second_factor",
    )(y2)
    image = jnp.concatenate([kx, kw], 1)
    at = (lax.axis_index("blk") * cols + q) * rows
    new_ritz, correction, norm2 = pl.pallas_call(
        general_last,
        out_shape=(shape(rows, width), shape(rows, width), shape(1, width)),
        in_specs=[VMEM] * 8,
        out_specs=(VMEM,) * 3,
        compiler_params=params(),
        name="last_step",
    )(
        y2,
        image,
        values,
        cross,
        factor2,
        lax.dynamic_slice_in_dim(y2, at, rows, 0),
        lax.dynamic_slice_in_dim(image, at, rows, 0),
        diag[:, None],
    )
    return new_ritz, correction, jnp.concatenate([norm1, norm2], 0)


def solution(mesh):
    n, cols = mesh.shape["blk"], mesh.shape["col"]
    placed = (
        P("blk", "col", None),
        P(("blk", "col"), None),
        P(("blk", "col"), None),
        P(("blk", "col")),
    )

    def per_device(kernel, ritz_block, search_block, precond_diag):
        rows = kernel[:, 0, :]
        if cols == 1 and n % 16 == 0 and ritz_block.shape[0] <= ritz_block.shape[1]:
            return ringed(n, rows, ritz_block, search_block, precond_diag)
        return general(n, cols, rows, ritz_block, search_block, precond_diag)

    return jax.shard_map(
        per_device,
        mesh=mesh,
        in_specs=placed,
        out_specs=(P(("blk", "col"), None), P(("blk", "col"), None), P()),
        check_vma=False,
    )
```

```python
import jax
import jax.numpy as jnp
from jax import lax
from jax.experimental import pallas as pl
from jax.experimental.pallas import tpu as pltpu
from jax.sharding import PartitionSpec as P

ITERS = 2
F32 = jnp.float32
BF16 = jnp.bfloat16
highest = lax.Precision.HIGHEST
CHUNK = 512


def params(mebibytes=56):
    return pltpu.CompilerParams(vmem_limit_bytes=mebibytes << 20)


def mm(a, b, ca=1, cb=0):
    return lax.dot_general(
        a, b, (((ca,), (cb,)), ((), ())), precision=highest, preferred_element_type=F32
    )


def halves(x):
    top = x.astype(BF16)
    return top, (x - top.astype(F32)).astype(BF16)


def mm3(a, b, ca=1, cb=0):
    a1, a2 = halves(a)
    b1, b2 = halves(b)
    return lax.dot_general(
        jnp.concatenate([a1, a1, a2], ca),
        jnp.concatenate([b1, b2, b1], cb),
        (((ca,), (cb,)), ((), ())),
        preferred_element_type=F32,
    )


def total_of(xs, ys):
    out = xs[0] * ys[0]
    for x, y in zip(xs[1:], ys[1:]):
        out = out + x * y
    return out


def solved(entry, columns):
    size = len(columns[0])
    if size == 2:
        x, y, z = entry(0, 0), entry(0, 1), entry(1, 1)
        scale = 1.0 / (x * z - y * y)
        q00, q01, q11 = z * scale, -(y * scale), x * scale
        return [[q00 * c[0] + q01 * c[1], q01 * c[0] + q11 * c[1]] for c in columns]
    h = size // 2
    side = [[entry(i, h + j) for i in range(h)] for j in range(h)]
    done = solved(entry, side + [c[:h] for c in columns])
    ties, upper = done[:h], done[h:]
    rest = {
        (i, j): entry(h + i, h + j) - total_of(side[i], ties[j])
        for j in range(h)
        for i in range(j + 1)
    }
    lower = solved(
        lambda i, j: rest[i, j],
        [[c[h + j] - total_of(ties[j], c[:h]) for j in range(h)] for c in columns],
    )
    return [
        [u[i] - total_of([ties[j][i] for j in range(h)], g) for i in range(h)] + g
        for u, g in zip(upper, lower)
    ]


def inverse_factor(matrix, panel=32, step=8):
    n = matrix.shape[0]
    lane = lax.broadcasted_iota(jnp.int32, (8, n), 1)
    sub = lax.broadcasted_iota(jnp.int32, (8, n), 0)
    a = [matrix[8 * v : 8 * v + 8, :] for v in range(n // 8)]

    def along(x, j):
        return jnp.broadcast_to(x[:, j : j + 1], (8, n))

    def down(x, i):
        return jnp.broadcast_to(x[i : i + 1, :], (8, n))

    rows = []
    for first in range(0, n, panel):
        last = (first + panel) // 8
        multipliers = []
        for k in range(first, first + panel, step):
            r = k // 8
            own = [along(a[r], k + j) for j in range(step)]
            pivot = {(i, j): down(own[j], i) for j in range(step) for i in range(j + 1)}
            inside = (lane >= k) & (lane < k + step)
            right = [
                jnp.where(lane == k + i, 1.0, jnp.where(inside, 0.0, down(a[r], i)))
                for i in range(step)
            ]
            g = solved(lambda i, j: pivot[i, j], [right])[0]
            finished, factor, norms = [], {}, []
            for i in range(step):
                y, d = right[i], pivot[i, i]
                for j in range(i):
                    e = pivot[j, i]
                    for m in range(j):
                        e = e - factor[i, m] * factor[j, m]
                    factor[i, j] = e * norms[j]
                for j in range(i):
                    d = d - factor[i, j] * factor[i, j]
                    y = y - factor[i, j] * finished[j]
                norms.append(lax.rsqrt(d))
                finished.append(y * norms[i])
            row, held = finished[0], g[0]
            for i in range(1, step):
                row = jnp.where(sub == i, finished[i], row)
                held = jnp.where(sub == i, g[i], held)
            rows.append(jnp.where(lane <= sub + k, row, 0.0))
            multipliers.append(
                jnp.where((lane >= k + step) & (lane < first + panel), 0.0, held)
            )
            for v in range(r + 1, last):
                other = [along(a[v], k + j) for j in range(step)]
                a[v] = jnp.where(inside, 0.0, a[v]) - total_of(other, g)
        if last < n // 8:
            change = mm(
                jnp.concatenate(a[first // 8 : last], 0), jnp.concatenate(multipliers, 0), 0, 0
            )
            inside = (lane >= first) & (lane < first + panel)
            for v in range(last, n // 8):
                a[v] = jnp.where(inside, 0.0, a[v]) - change[8 * v : 8 * v + 8]
    return jnp.concatenate(rows, 0)


def layout_of(rings):
    far = [8 * z for z in range(1, rings)]
    chips = [[0, 2, 4, 6], far] + [[d ^ m for d in far] for m in (2, 4, 6)]
    return chips + [[d ^ 1 for d in piece] for piece in chips]


def pack_blocks(*refs):
    parts, out_ref = refs[:-1], refs[-1]
    at = 0
    for part in parts:
        out_ref[at : at + part.shape[0], :] = part[...]
        at += part.shape[0]


def packed(parts, name):
    rows = sum(part.shape[0] for part in parts)
    with jax.named_scope(name):
        return pl.pallas_call(
            pack_blocks,
            out_shape=shape(rows, parts[0].shape[1]),
            in_specs=[VMEM] * len(parts),
            out_specs=VMEM,
            compiler_params=params(2),
            cost_estimate=cost(0.5),
            name=name,
        )(*parts)


def gather(block, n, tag):
    def swap(x, m, name):
        with jax.named_scope(tag + name):
            return lax.ppermute(x, "blk", [(i, i ^ m) for i in range(n)])

    far = [swap(block, 8 * z, f"_z{z}") for z in range(n // 8 - 1, 0, -1)][::-1]
    near = [block] + [swap(block, 2 * k, f"_n{k}") for k in (3, 1, 2)]
    near = [near[0], near[2], near[3], near[1]]
    column = packed(far, tag + "_column")
    corner = swap(column, 6, "_c3")
    chips = [packed(near, tag + "_near"), column, swap(column, 2, "_c1"), swap(column, 4, "_c2"), corner]
    return chips + [swap(x, 1, f"_core{i}") for i, x in enumerate(chips)]


def assemble(me, pieces, rings, place):
    for piece, distances in zip(pieces, layout_of(rings)):
        for slot, distance in enumerate(distances):
            place(piece, slot, jnp.bitwise_xor(me, distance))


def first_product(rings, rows, me_ref, kernel_ref, diag_ref, *refs):
    pieces, (y_ref, ky_ref) = refs[:-2], refs[-2:]
    width = y_ref.shape[1] // 2

    def place(piece, slot, device):
        base = slot * 2 * rows
        at = pl.ds(pl.multiple_of(device * rows, rows), rows)
        y_ref[at, :width] = piece[base : base + rows, :]
        y_ref[at, width:] = piece[base + rows : base + 2 * rows, :]

    assemble(me_ref[0], pieces, rings, place)
    result = mm3(kernel_ref[...], y_ref[...])
    ky_ref[:rows, :] = result[:, :width]
    ky_ref[rows : 2 * rows, :] = result[:, width:]
    ky_ref[2 * rows :, :] = jnp.broadcast_to(diag_ref[...], (8, width))


def metric_head(y_ref, metric_ref, upper_ref):
    total, double = y_ref.shape
    width = double // 2
    chunk = min(CHUNK, total)

    def add(i, acc):
        part = y_ref[pl.ds(pl.multiple_of(i * chunk, chunk), chunk), :]
        return acc + mm3(part, part, 0, 0)

    metric = lax.fori_loop(0, total // chunk, add, jnp.zeros((double, double), F32))
    metric_ref[...] = metric
    upper_ref[...] = inverse_factor(metric[:width, :width])


def metric_tail(metric_ref, upper_ref, out_ref):
    width = upper_ref.shape[0]
    upper = upper_ref[...]
    cross = mm(upper, metric_ref[:width, width:])
    lower = inverse_factor(metric_ref[width:, width:] - mm(cross, cross, 0, 0))
    out_ref[:width, :width] = upper
    out_ref[:width, width:] = jnp.zeros((width, width), F32)
    out_ref[width:, :width] = -mm(lower, mm(cross, upper, 0, 0))
    out_ref[width:, width:] = lower


def divided(residual, diag, values):
    eye = lax.broadcasted_iota(jnp.int32, values.shape, 0) == lax.broadcasted_iota(
        jnp.int32, values.shape, 1
    )
    level = jnp.sum(jnp.where(eye, values, 0.0), axis=0, keepdims=True)
    return residual / jnp.maximum(jnp.abs(diag - level), 1.0)


def first_step(y_ref, ky_ref, factor_ref, diag_ref, y2_ref, kx_ref, small_ref, norm_ref):
    total, double = y_ref.shape
    width = double // 2
    rows = diag_ref.shape[0]
    chunk = min(CHUNK, total)

    def add(i, acc):
        at = pl.ds(pl.multiple_of(i * chunk, chunk), chunk)
        return acc + mm3(y_ref[at, :], ky_ref[at, :], 0, 0)

    g = lax.fori_loop(0, total // chunk, add, jnp.zeros((double, double), F32))
    factor = factor_ref[...]
    head = g[:width, :]
    side = jnp.concatenate([g[:width, :width], g[:width, width:].T], 0)
    whole = jnp.concatenate(
        [head, jnp.concatenate([g[:width, width:].T, g[width:, width:]], 1)], 0
    )
    z = mm(factor, side)
    small = inverse_factor(mm(z, z, 0, 0))
    mixing = mm(factor, mm(z, small, 1, 1), 0, 0)
    values = mm(mixing, mm(whole, mixing), 0, 0)
    both = jnp.concatenate([mixing, mm(mixing, values)], 1)
    small_ref[...] = values

    def update(i, acc):
        at = pl.ds(pl.multiple_of(i * chunk, chunk), chunk)
        pair = mm3(y_ref[at, :], both)
        image = mm3(ky_ref[at, :], mixing)
        y2_ref[at, :width] = pair[:, :width]
        kx_ref[at, :] = image
        residual = image - pair[:, width:]
        y2_ref[at, width:] = residual
        return acc + jnp.sum(residual * residual, axis=0, keepdims=True)

    squares = lax.fori_loop(0, total // chunk, update, jnp.zeros((1, width), F32))
    norm_ref[...] = jnp.sqrt(squares)
    for b in range(total // rows):
        at = pl.ds(b * rows, rows)
        y2_ref[at, width:] = divided(y2_ref[at, width:], diag_ref[:rows, b : b + 1], values)


def with_product(rings, rows, me_ref, kernel_ref, y_ref, factor_ref, *refs):
    pieces = refs[:-8]
    y2_ref, kx_ref, small_ref, norm_ref, kw_ref, ky_ref, table, diag_ref = refs[-8:]
    width = kx_ref.shape[1]
    step = 2 * rows + 8

    def place(piece, slot, device):
        base = slot * step
        at = pl.ds(pl.multiple_of(device * rows, rows), rows)
        ky_ref[at, :width] = piece[base : base + rows, :]
        ky_ref[at, width:] = piece[base + rows : base + 2 * rows, :]
        table[pl.ds(device, 1), :] = piece[base + 2 * rows : base + 2 * rows + 1, :]

    table[...] = jnp.zeros_like(table)
    assemble(me_ref[0], pieces, rings, place)
    diag_ref[...] = table[...].T
    first_step(
        y_ref, ky_ref, factor_ref, diag_ref.at[:rows, :], y2_ref, kx_ref, small_ref, norm_ref
    )
    kw_ref[...] = mm3(kernel_ref[...], y2_ref[:, width:])


def second_factor(y2_ref, gram_ref, factor_ref):
    total, double = y2_ref.shape
    width = double // 2
    chunk = min(CHUNK, total)

    def add(i, acc):
        at = pl.ds(pl.multiple_of(i * chunk, chunk), chunk)
        return acc + mm3(y2_ref[at, :], y2_ref[at, width:], 0, 0)

    gram = lax.fori_loop(0, total // chunk, add, jnp.zeros((double, width), F32))
    cross = gram[:width]
    gram_ref[...] = cross
    factor_ref[...] = inverse_factor(gram[width:] - mm(cross, cross, 0, 0))


def second_step(
    y2_ref, image_ref, small_ref, cross_ref, factor_ref, own_y2, own_image, own_diag, outs
):
    ritz_ref, search_ref, norm_ref = outs
    total, double = y2_ref.shape
    width = double // 2
    chunk = min(CHUNK, total)

    def add(i, acc):
        at = pl.ds(pl.multiple_of(i * chunk, chunk), chunk)
        return acc + mm3(y2_ref[at, :], image_ref[at, width:], 0, 0)

    g = lax.fori_loop(0, total // chunk, add, jnp.zeros((double, width), F32))
    values, cross, factor = small_ref[...], cross_ref[...], factor_ref[...]
    f_t = g[:width].T
    z = mm(factor, f_t - mm(cross, values, 0, 0))
    small = inverse_factor(mm(values, values, 0, 0) + mm(z, z, 0, 0))
    lower = mm(factor, mm(z, small, 1, 1), 0, 0)
    upper = mm(values, small, 1, 1) - mm(cross, lower)
    mixing = jnp.concatenate([upper, lower], 0)
    whole = jnp.concatenate(
        [jnp.concatenate([values, g[:width]], 1), jnp.concatenate([f_t, g[width:]], 1)], 0
    )
    values2 = mm(mixing, mm(whole, mixing), 0, 0)
    turned = mm(mixing, values2)

    def update(i, acc):
        at = pl.ds(pl.multiple_of(i * chunk, chunk), chunk)
        residual = mm3(image_ref[at, :], mixing) - mm3(y2_ref[at, :], turned)
        return acc + jnp.sum(residual * residual, axis=0, keepdims=True)

    squares = lax.fori_loop(0, total // chunk, update, jnp.zeros((1, width), F32))
    norm_ref[...] = jnp.sqrt(squares)
    own = own_y2()
    ritz = mm(own, mixing)
    ritz_ref[...] = ritz
    residual = mm(own_image(), mixing) - mm(ritz, values2)
    search_ref[...] = divided(residual, own_diag(), values2)


def last_step(rings, rows, me_ref, y2_ref, kx_ref, small_ref, cross_ref, factor_ref, own_ref, *refs):
    pieces = refs[:-4]
    ritz_ref, search_ref, norm_ref, image_ref = refs[-4:]
    width = kx_ref.shape[1]
    me = me_ref[0]

    def place(piece, slot, device):
        at = pl.ds(pl.multiple_of(device * rows, rows), rows)
        image_ref[at, width:] = piece[slot * rows : (slot + 1) * rows, :]

    assemble(me, pieces, rings, place)
    image_ref[:, :width] = kx_ref[...]
    mine = pl.ds(pl.multiple_of(me * rows, rows), rows)
    second_step(
        y2_ref,
        image_ref,
        small_ref,
        cross_ref,
        factor_ref,
        lambda: y2_ref[mine, :],
        lambda: image_ref[mine, :],
        lambda: own_ref[...],
        (ritz_ref, search_ref, norm_ref),
    )


def general_last(y2_ref, image_ref, small_ref, cross_ref, factor_ref, own_y2, own_image, own_diag, *outs):
    second_step(
        y2_ref,
        image_ref,
        small_ref,
        cross_ref,
        factor_ref,
        lambda: own_y2[...],
        lambda: own_image[...],
        lambda: own_diag[...],
        outs,
    )


def cost(us):
    return pl.CostEstimate(flops=int(us * 1e9), bytes_accessed=0, transcendentals=0)


def shape(*dims):
    return jax.ShapeDtypeStruct(dims, F32)


VMEM = pl.BlockSpec(memory_space=pltpu.VMEM)
SMEM = pl.BlockSpec(memory_space=pltpu.SMEM)


def metric_factor(y, mebibytes):
    width = y.shape[1] // 2
    with jax.named_scope("metric_head"):
        metric, upper = pl.pallas_call(
            metric_head,
            out_shape=(shape(2 * width, 2 * width), shape(width, width)),
            in_specs=[VMEM],
            out_specs=(VMEM, VMEM),
            compiler_params=params(mebibytes),
            cost_estimate=cost(7),
            name="metric_head",
        )(y)
    with jax.named_scope("metric_tail"):
        return pl.pallas_call(
            metric_tail,
            out_shape=shape(2 * width, 2 * width),
            in_specs=[VMEM, VMEM],
            out_specs=VMEM,
            compiler_params=params(mebibytes),
            cost_estimate=cost(7),
            name="metric_tail",
        )(metric, upper)


def second_metric(y2, mebibytes):
    width = y2.shape[1] // 2
    with jax.named_scope("second_factor"):
        return pl.pallas_call(
            second_factor,
            out_shape=(shape(width, width), shape(width, width)),
            in_specs=[VMEM],
            out_specs=(VMEM, VMEM),
            compiler_params=params(mebibytes),
            cost_estimate=cost(9),
            name="second_factor",
        )(y2)


def cubed(n, kernel, ritz, search, diag):
    rows, width = ritz.shape
    rings = n // 8
    total = n * rows
    lanes = max(n, 128)
    me = lax.axis_index("blk").astype(jnp.int32).reshape(1)
    along = jnp.zeros((1, width), F32).at[0, :rows].set(diag)
    sent = gather(jnp.concatenate([ritz, search], 0), n, "ag1")
    y, ky_own = pl.pallas_call(
        lambda *refs: first_product(rings, rows, *refs),
        out_shape=(shape(total, 2 * width), shape(2 * rows + 8, width)),
        in_specs=[SMEM, VMEM, VMEM] + [VMEM] * len(sent),
        out_specs=(VMEM, VMEM),
        compiler_params=params(16),
        name="first_product",
    )(me, kernel, along, *sent)
    images = gather(ky_own, n, "ag2")
    factor = metric_factor(y, 12)
    y2, kx, values, norm1, kw_own = pl.pallas_call(
        lambda *refs: with_product(rings, rows, *refs),
        out_shape=(
            shape(total, 2 * width),
            shape(total, width),
            shape(width, width),
            shape(1, width),
            shape(rows, width),
        ),
        in_specs=[SMEM] + [VMEM] * (3 + len(images)),
        out_specs=(VMEM,) * 5,
        scratch_shapes=[
            pltpu.VMEM((total, 2 * width), F32),
            pltpu.VMEM((lanes, width), F32),
            pltpu.VMEM((width, lanes), F32),
        ],
        compiler_params=params(24),
        name="first_step",
    )(me, kernel, y, factor, *images)
    images2 = gather(kw_own, n, "ag3")
    cross, factor2 = second_metric(y2, 12)
    new_ritz, correction, norm2 = pl.pallas_call(
        lambda *refs: last_step(rings, rows, *refs),
        out_shape=(shape(rows, width), shape(rows, width), shape(1, width)),
        in_specs=[SMEM] + [VMEM] * (6 + len(images2)),
        out_specs=(VMEM,) * 3,
        scratch_shapes=[pltpu.VMEM((total, 2 * width), F32)],
        compiler_params=params(24),
        name="last_step",
    )(me, y2, kx, values, cross, factor2, diag[:, None], *images2)
    return new_ritz, correction, jnp.concatenate([norm1, norm2], 0)


def general(n, cols, kernel, ritz, search, diag):
    rows, width = ritz.shape
    axes = ("blk", "col")
    total = n * cols * rows
    q = lax.axis_index("col")

    def product(part):
        whole = lax.psum_scatter(mm(kernel, part), "col", scatter_dimension=0, tiled=True)
        return whole

    own = jnp.concatenate([ritz, search], 1)
    part = lax.all_gather(own, "blk", axis=0, tiled=True)
    y = lax.all_gather(own, axes, axis=0, tiled=True)
    ky = lax.all_gather(product(part), axes, axis=0, tiled=True)
    table = lax.all_gather(diag, axes, axis=0, tiled=True).reshape(n * cols, rows).T
    factor = metric_factor(y, 56)
    y2, kx, values, norm1 = pl.pallas_call(
        first_step,
        out_shape=(shape(total, 2 * width), shape(total, width), shape(width, width), shape(1, width)),
        in_specs=[VMEM] * 4,
        out_specs=(VMEM,) * 4,
        compiler_params=params(),
        name="first_step",
    )(y, ky, factor, table)
    held = y2[:, width:].reshape(n, cols, rows, width)
    part2 = lax.dynamic_index_in_dim(held, q, 1, keepdims=False).reshape(n * rows, width)
    kw = lax.all_gather(product(part2), axes, axis=0, tiled=True)
    cross, factor2 = second_metric(y2, 56)
    image = jnp.concatenate([kx, kw], 1)
    at = (lax.axis_index("blk") * cols + q) * rows
    new_ritz, correction, norm2 = pl.pallas_call(
        general_last,
        out_shape=(shape(rows, width), shape(rows, width), shape(1, width)),
        in_specs=[VMEM] * 8,
        out_specs=(VMEM,) * 3,
        compiler_params=params(),
        name="last_step",
    )(
        y2,
        image,
        values,
        cross,
        factor2,
        lax.dynamic_slice_in_dim(y2, at, rows, 0),
        lax.dynamic_slice_in_dim(image, at, rows, 0),
        diag[:, None],
    )
    return new_ritz, correction, jnp.concatenate([norm1, norm2], 0)


def solution(mesh):
    n, cols = mesh.shape["blk"], mesh.shape["col"]
    placed = (
        P("blk", "col", None),
        P(("blk", "col"), None),
        P(("blk", "col"), None),
        P(("blk", "col")),
    )

    def per_device(kernel, ritz_block, search_block, precond_diag):
        rows = kernel[:, 0, :]
        if cols == 1 and n >= 16 and n & (n - 1) == 0 and ritz_block.shape[0] <= ritz_block.shape[1]:
            return cubed(n, rows, ritz_block, search_block, precond_diag)
        return general(n, cols, rows, ritz_block, search_block, precond_diag)

    return jax.shard_map(
        per_device,
        mesh=mesh,
        in_specs=placed,
        out_specs=(P(("blk", "col"), None), P(("blk", "col"), None), P()),
        check_vma=False,
    )
```

```python
import jax
import jax.numpy as jnp
from jax import lax
from jax.experimental import pallas as pl
from jax.experimental.pallas import tpu as pltpu
from jax.sharding import PartitionSpec as P


ITERS = 2
F32 = jnp.float32
BF16 = jnp.bfloat16
highest = lax.Precision.HIGHEST
CHUNK = 512


def params(mebibytes=56):
    return pltpu.CompilerParams(vmem_limit_bytes=mebibytes << 20)


def mm(a, b, ca=1, cb=0):
    return lax.dot_general(
        a, b, (((ca,), (cb,)), ((), ())), precision=highest, preferred_element_type=F32
    )


def halves(x):
    top = x.astype(BF16)
    return top, (x - top.astype(F32)).astype(BF16)


def mm3(a, b, ca=1, cb=0):
    a1, a2 = halves(a)
    b1, b2 = halves(b)
    return lax.dot_general(
        jnp.concatenate([a1, a1, a2], ca),
        jnp.concatenate([b1, b2, b1], cb),
        (((ca,), (cb,)), ((), ())),
        preferred_element_type=F32,
    )


def total_of(xs, ys):
    out = xs[0] * ys[0]
    for x, y in zip(xs[1:], ys[1:]):
        out = out + x * y
    return out


def solved(entry, columns):
    size = len(columns[0])
    if size == 2:
        x, y, z = entry(0, 0), entry(0, 1), entry(1, 1)
        scale = 1.0 / (x * z - y * y)
        q00, q01, q11 = z * scale, -(y * scale), x * scale
        return [[q00 * c[0] + q01 * c[1], q01 * c[0] + q11 * c[1]] for c in columns]
    h = size // 2
    side = [[entry(i, h + j) for i in range(h)] for j in range(h)]
    done = solved(entry, side + [c[:h] for c in columns])
    ties, upper = done[:h], done[h:]
    rest = {
        (i, j): entry(h + i, h + j) - total_of(side[i], ties[j])
        for j in range(h)
        for i in range(j + 1)
    }
    lower = solved(
        lambda i, j: rest[i, j],
        [[c[h + j] - total_of(ties[j], c[:h]) for j in range(h)] for c in columns],
    )
    return [
        [u[i] - total_of([ties[j][i] for j in range(h)], g) for i in range(h)] + g
        for u, g in zip(upper, lower)
    ]


def inverse_factor(matrix, panel=32, step=8):
    n = matrix.shape[0]
    lane = lax.broadcasted_iota(jnp.int32, (8, n), 1)
    sub = lax.broadcasted_iota(jnp.int32, (8, n), 0)
    a = [matrix[8 * v : 8 * v + 8, :] for v in range(n // 8)]

    def along(x, j):
        return jnp.broadcast_to(x[:, j : j + 1], (8, n))

    def down(x, i):
        return jnp.broadcast_to(x[i : i + 1, :], (8, n))

    rows = []
    for first in range(0, n, panel):
        last = (first + panel) // 8
        multipliers = []
        for k in range(first, first + panel, step):
            r = k // 8
            own = [along(a[r], k + j) for j in range(step)]
            pivot = {(i, j): down(own[j], i) for j in range(step) for i in range(j + 1)}
            inside = (lane >= k) & (lane < k + step)
            right = [
                jnp.where(lane == k + i, 1.0, jnp.where(inside, 0.0, down(a[r], i)))
                for i in range(step)
            ]
            g = solved(lambda i, j: pivot[i, j], [right])[0]
            finished, factor, norms = [], {}, []
            for i in range(step):
                y, d = right[i], pivot[i, i]
                for j in range(i):
                    e = pivot[j, i]
                    for m in range(j):
                        e = e - factor[i, m] * factor[j, m]
                    factor[i, j] = e * norms[j]
                for j in range(i):
                    d = d - factor[i, j] * factor[i, j]
                    y = y - factor[i, j] * finished[j]
                norms.append(lax.rsqrt(d))
                finished.append(y * norms[i])
            row, held = finished[0], g[0]
            for i in range(1, step):
                row = jnp.where(sub == i, finished[i], row)
                held = jnp.where(sub == i, g[i], held)
            rows.append(jnp.where(lane <= sub + k, row, 0.0))
            multipliers.append(
                jnp.where((lane >= k + step) & (lane < first + panel), 0.0, held)
            )
            for v in range(r + 1, last):
                other = [along(a[v], k + j) for j in range(step)]
                a[v] = jnp.where(inside, 0.0, a[v]) - total_of(other, g)
        if last < n // 8:
            change = mm(
                jnp.concatenate(a[first // 8 : last], 0), jnp.concatenate(multipliers, 0), 0, 0
            )
            inside = (lane >= first) & (lane < first + panel)
            for v in range(last, n // 8):
                a[v] = jnp.where(inside, 0.0, a[v]) - change[8 * v : 8 * v + 8]
    return jnp.concatenate(rows, 0)


def layout_of(rings):
    column = [8 * z for z in range(rings)]
    chips = [[d ^ m for d in column] for m in (0, 2, 4, 6)]
    return chips + [[d ^ 1 for d in piece] for piece in chips]


def pack_blocks(*refs):
    parts, out_ref = refs[:-1], refs[-1]
    at = 0
    for part in parts:
        out_ref[at : at + part.shape[0], :] = part[...]
        at += part.shape[0]


def packed(parts):
    rows = sum(part.shape[0] for part in parts)
    return pl.pallas_call(
        pack_blocks,
        out_shape=shape(rows, parts[0].shape[1]),
        in_specs=[VMEM] * len(parts),
        out_specs=VMEM,
        compiler_params=params(2),
        cost_estimate=cost(0.5),
    )(*parts)


def gather(block, n):
    def swap(x, m):
        return lax.ppermute(x, "blk", [(i, i ^ m) for i in range(n)])

    column = packed([block] + [swap(block, 8 * z) for z in range(1, n // 8)])
    chips = [column] + [swap(column, 2 * k) for k in (1, 2, 3)]
    return chips + [swap(x, 1) for x in chips]


def assemble(me, pieces, rings, place):
    for piece, distances in zip(pieces, layout_of(rings)):
        for slot, distance in enumerate(distances):
            place(piece, slot, jnp.bitwise_xor(me, distance))


def first_product(rings, rows, me_ref, kernel_ref, diag_ref, *refs):
    pieces, (y_ref, ky_ref) = refs[:-2], refs[-2:]
    width = y_ref.shape[1] // 2

    def place(piece, slot, device):
        base = slot * 2 * rows
        at = pl.ds(pl.multiple_of(device * rows, rows), rows)
        y_ref[at, :width] = piece[base : base + rows, :]
        y_ref[at, width:] = piece[base + rows : base + 2 * rows, :]

    assemble(me_ref[0], pieces, rings, place)
    result = mm3(kernel_ref[...], y_ref[...])
    ky_ref[:rows, :] = result[:, :width]
    ky_ref[rows : 2 * rows, :] = result[:, width:]
    ky_ref[2 * rows :, :] = jnp.zeros((8, width), F32)
    ky_ref[2 * rows : 2 * rows + 1, :rows] = diag_ref[...]


def metric_head(y_ref, metric_ref, upper_ref):
    total, double = y_ref.shape
    width = double // 2
    chunk = min(CHUNK, total)

    def add(i, acc):
        part = y_ref[pl.ds(pl.multiple_of(i * chunk, chunk), chunk), :]
        return acc + mm3(part, part, 0, 0)

    metric = lax.fori_loop(0, total // chunk, add, jnp.zeros((double, double), F32))
    metric_ref[...] = metric
    upper_ref[...] = inverse_factor(metric[:width, :width])


def metric_tail(metric_ref, upper_ref, out_ref):
    width = upper_ref.shape[0]
    upper = upper_ref[...]
    cross = mm(upper, metric_ref[:width, width:])
    lower = inverse_factor(metric_ref[width:, width:] - mm(cross, cross, 0, 0))
    out_ref[:width, :width] = upper
    out_ref[:width, width:] = jnp.zeros((width, width), F32)
    out_ref[width:, :width] = -mm(lower, mm(cross, upper, 0, 0))
    out_ref[width:, width:] = lower


def divided(residual, diag, values):
    eye = lax.broadcasted_iota(jnp.int32, values.shape, 0) == lax.broadcasted_iota(
        jnp.int32, values.shape, 1
    )
    level = jnp.sum(jnp.where(eye, values, 0.0), axis=0, keepdims=True)
    return residual / jnp.maximum(jnp.abs(diag - level), 1.0)


def first_step(y_ref, ky_ref, factor_ref, diag_ref, y2_ref, kx_ref, small_ref, norm_ref):
    total, double = y_ref.shape
    width = double // 2
    rows = diag_ref.shape[0]
    chunk = min(CHUNK, total)

    def add(i, acc):
        at = pl.ds(pl.multiple_of(i * chunk, chunk), chunk)
        return acc + mm3(y_ref[at, :], ky_ref[at, :], 0, 0)

    g = lax.fori_loop(0, total // chunk, add, jnp.zeros((double, double), F32))
    factor = factor_ref[...]
    head = g[:width, :]
    side = jnp.concatenate([g[:width, :width], g[:width, width:].T], 0)
    whole = jnp.concatenate(
        [head, jnp.concatenate([g[:width, width:].T, g[width:, width:]], 1)], 0
    )
    z = mm(factor, side)
    small = inverse_factor(mm(z, z, 0, 0))
    mixing = mm(factor, mm(z, small, 1, 1), 0, 0)
    values = mm(mixing, mm(whole, mixing), 0, 0)
    both = jnp.concatenate([mixing, mm(mixing, values)], 1)
    small_ref[...] = values

    def update(i, acc):
        at = pl.ds(pl.multiple_of(i * chunk, chunk), chunk)
        pair = mm3(y_ref[at, :], both)
        image = mm3(ky_ref[at, :], mixing)
        y2_ref[at, :width] = pair[:, :width]
        kx_ref[at, :] = image
        residual = image - pair[:, width:]
        y2_ref[at, width:] = residual
        return acc + jnp.sum(residual * residual, axis=0, keepdims=True)

    squares = lax.fori_loop(0, total // chunk, update, jnp.zeros((1, width), F32))
    norm_ref[...] = jnp.sqrt(squares)
    for b in range(total // rows):
        at = pl.ds(b * rows, rows)
        y2_ref[at, width:] = divided(y2_ref[at, width:], diag_ref[:rows, b : b + 1], values)


def with_product(rings, rows, me_ref, kernel_ref, y_ref, factor_ref, *refs):
    pieces = refs[:-8]
    y2_ref, kx_ref, small_ref, norm_ref, kw_ref, ky_ref, table, diag_ref = refs[-8:]
    width = kx_ref.shape[1]
    step = 2 * rows + 8

    def place(piece, slot, device):
        base = slot * step
        at = pl.ds(pl.multiple_of(device * rows, rows), rows)
        ky_ref[at, :width] = piece[base : base + rows, :]
        ky_ref[at, width:] = piece[base + rows : base + 2 * rows, :]
        table[pl.ds(device, 1), :] = piece[base + 2 * rows : base + 2 * rows + 1, :]

    table[...] = jnp.zeros_like(table)
    assemble(me_ref[0], pieces, rings, place)
    diag_ref[...] = table[...].T
    first_step(
        y_ref, ky_ref, factor_ref, diag_ref.at[:rows, :], y2_ref, kx_ref, small_ref, norm_ref
    )
    kw_ref[...] = mm3(kernel_ref[...], y2_ref[:, width:])


def second_factor(y2_ref, gram_ref, factor_ref):
    total, double = y2_ref.shape
    width = double // 2
    chunk = min(CHUNK, total)

    def add(i, acc):
        at = pl.ds(pl.multiple_of(i * chunk, chunk), chunk)
        return acc + mm3(y2_ref[at, :], y2_ref[at, width:], 0, 0)

    gram = lax.fori_loop(0, total // chunk, add, jnp.zeros((double, width), F32))
    cross = gram[:width]
    gram_ref[...] = cross
    factor_ref[...] = inverse_factor(gram[width:] - mm(cross, cross, 0, 0))


def second_step(
    y2_ref, image_ref, small_ref, cross_ref, factor_ref, first_ref, own_y2, own_image, own_diag, outs
):
    ritz_ref, search_ref, norm_ref = outs
    total, double = y2_ref.shape
    width = double // 2
    chunk = min(CHUNK, total)

    def add(i, acc):
        at = pl.ds(pl.multiple_of(i * chunk, chunk), chunk)
        return acc + mm3(y2_ref[at, :], image_ref[at, width:], 0, 0)

    g = lax.fori_loop(0, total // chunk, add, jnp.zeros((double, width), F32))
    values, cross, factor = small_ref[...], cross_ref[...], factor_ref[...]
    f_t = g[:width].T
    z = mm(factor, f_t - mm(cross, values, 0, 0))
    small = inverse_factor(mm(values, values, 0, 0) + mm(z, z, 0, 0))
    lower = mm(factor, mm(z, small, 1, 1), 0, 0)
    upper = mm(values, small, 1, 1) - mm(cross, lower)
    mixing = jnp.concatenate([upper, lower], 0)
    whole = jnp.concatenate(
        [jnp.concatenate([values, g[:width]], 1), jnp.concatenate([f_t, g[width:]], 1)], 0
    )
    values2 = mm(mixing, mm(whole, mixing), 0, 0)
    turned = mm(mixing, values2)

    def update(i, acc):
        at = pl.ds(pl.multiple_of(i * chunk, chunk), chunk)
        residual = mm3(image_ref[at, :], mixing) - mm3(y2_ref[at, :], turned)
        return acc + jnp.sum(residual * residual, axis=0, keepdims=True)

    squares = lax.fori_loop(0, total // chunk, update, jnp.zeros((1, width), F32))
    norm_ref[:1, :] = first_ref[...]
    norm_ref[1:, :] = jnp.sqrt(squares)
    own = own_y2()
    ritz = mm(own, mixing)
    ritz_ref[...] = ritz
    residual = mm(own_image(), mixing) - mm(ritz, values2)
    search_ref[...] = divided(residual, own_diag(), values2)


def last_step(rings, rows, me_ref, y2_ref, kx_ref, small_ref, cross_ref, factor_ref, first_ref, diag_ref, *refs):
    pieces = refs[:-4]
    ritz_ref, search_ref, norm_ref, image_ref = refs[-4:]
    width = kx_ref.shape[1]
    me = me_ref[0]

    def place(piece, slot, device):
        at = pl.ds(pl.multiple_of(device * rows, rows), rows)
        image_ref[at, width:] = piece[slot * rows : (slot + 1) * rows, :]

    assemble(me, pieces, rings, place)
    image_ref[:, :width] = kx_ref[...]
    mine = pl.ds(pl.multiple_of(me * rows, rows), rows)
    second_step(
        y2_ref,
        image_ref,
        small_ref,
        cross_ref,
        factor_ref,
        first_ref,
        lambda: y2_ref[mine, :],
        lambda: image_ref[mine, :],
        lambda: jnp.broadcast_to(diag_ref[...], (8, rows)).T[:, :1],
        (ritz_ref, search_ref, norm_ref),
    )


def general_last(
    y2_ref, image_ref, small_ref, cross_ref, factor_ref, first_ref, own_y2, own_image, own_diag, *outs
):
    second_step(
        y2_ref,
        image_ref,
        small_ref,
        cross_ref,
        factor_ref,
        first_ref,
        lambda: own_y2[...],
        lambda: own_image[...],
        lambda: own_diag[...],
        outs,
    )


def cost(us):
    return pl.CostEstimate(flops=int(us * 1e9), bytes_accessed=0, transcendentals=0)


def shape(*dims):
    return jax.ShapeDtypeStruct(dims, F32)


VMEM = pl.BlockSpec(memory_space=pltpu.VMEM)
SMEM = pl.BlockSpec(memory_space=pltpu.SMEM)


def metric_factor(y, mebibytes):
    width = y.shape[1] // 2
    metric, upper = pl.pallas_call(
        metric_head,
        out_shape=(shape(2 * width, 2 * width), shape(width, width)),
        in_specs=[VMEM],
        out_specs=(VMEM, VMEM),
        compiler_params=params(mebibytes),
        cost_estimate=cost(7),
        name="metric_head",
    )(y)
    return pl.pallas_call(
        metric_tail,
        out_shape=shape(2 * width, 2 * width),
        in_specs=[VMEM, VMEM],
        out_specs=VMEM,
        compiler_params=params(mebibytes),
        cost_estimate=cost(7),
        name="metric_tail",
    )(metric, upper)


def second_metric(y2, mebibytes):
    width = y2.shape[1] // 2
    return pl.pallas_call(
        second_factor,
        out_shape=(shape(width, width), shape(width, width)),
        in_specs=[VMEM],
        out_specs=(VMEM, VMEM),
        compiler_params=params(mebibytes),
        cost_estimate=cost(9),
        name="second_factor",
    )(y2)


def cubed(n, kernel, ritz, search, diag):
    rows, width = ritz.shape
    rings = n // 8
    total = n * rows
    lanes = max(n, 128)
    me = lax.axis_index("blk").astype(jnp.int32).reshape(1)
    along = diag.reshape(1, rows)
    sent = gather(packed([ritz, search]), n)
    y, ky_own = pl.pallas_call(
        lambda *refs: first_product(rings, rows, *refs),
        out_shape=(shape(total, 2 * width), shape(2 * rows + 8, width)),
        in_specs=[SMEM, VMEM, VMEM] + [VMEM] * len(sent),
        out_specs=(VMEM, VMEM),
        compiler_params=params(16),
        name="first_product",
    )(me, kernel, along, *sent)
    images = gather(ky_own, n)
    factor = metric_factor(y, 12)
    y2, kx, values, norm1, kw_own = pl.pallas_call(
        lambda *refs: with_product(rings, rows, *refs),
        out_shape=(
            shape(total, 2 * width),
            shape(total, width),
            shape(width, width),
            shape(1, width),
            shape(rows, width),
        ),
        in_specs=[SMEM] + [VMEM] * (3 + len(images)),
        out_specs=(VMEM,) * 5,
        scratch_shapes=[
            pltpu.VMEM((total, 2 * width), F32),
            pltpu.VMEM((lanes, width), F32),
            pltpu.VMEM((width, lanes), F32),
        ],
        compiler_params=params(24),
        name="first_step",
    )(me, kernel, y, factor, *images)
    images2 = gather(kw_own, n)
    cross, factor2 = second_metric(y2, 12)
    return pl.pallas_call(
        lambda *refs: last_step(rings, rows, *refs),
        out_shape=(shape(rows, width), shape(rows, width), shape(ITERS, width)),
        in_specs=[SMEM] + [VMEM] * (7 + len(images2)),
        out_specs=(VMEM,) * 3,
        scratch_shapes=[pltpu.VMEM((total, 2 * width), F32)],
        compiler_params=params(24),
        name="last_step",
    )(me, y2, kx, values, cross, factor2, norm1, along, *images2)


def general(n, cols, kernel, ritz, search, diag):
    rows, width = ritz.shape
    axes = ("blk", "col")
    total = n * cols * rows
    q = lax.axis_index("col")

    def product(part):
        whole = lax.psum_scatter(mm(kernel, part), "col", scatter_dimension=0, tiled=True)
        return whole

    own = jnp.concatenate([ritz, search], 1)
    part = lax.all_gather(own, "blk", axis=0, tiled=True)
    y = lax.all_gather(own, axes, axis=0, tiled=True)
    ky = lax.all_gather(product(part), axes, axis=0, tiled=True)
    table = lax.all_gather(diag, axes, axis=0, tiled=True).reshape(n * cols, rows).T
    factor = metric_factor(y, 56)
    y2, kx, values, norm1 = pl.pallas_call(
        first_step,
        out_shape=(shape(total, 2 * width), shape(total, width), shape(width, width), shape(1, width)),
        in_specs=[VMEM] * 4,
        out_specs=(VMEM,) * 4,
        compiler_params=params(),
        name="first_step",
    )(y, ky, factor, table)
    held = y2[:, width:].reshape(n, cols, rows, width)
    part2 = lax.dynamic_index_in_dim(held, q, 1, keepdims=False).reshape(n * rows, width)
    kw = lax.all_gather(product(part2), axes, axis=0, tiled=True)
    cross, factor2 = second_metric(y2, 56)
    image = jnp.concatenate([kx, kw], 1)
    at = (lax.axis_index("blk") * cols + q) * rows
    return pl.pallas_call(
        general_last,
        out_shape=(shape(rows, width), shape(rows, width), shape(ITERS, width)),
        in_specs=[VMEM] * 9,
        out_specs=(VMEM,) * 3,
        compiler_params=params(),
        name="last_step",
    )(
        y2,
        image,
        values,
        cross,
        factor2,
        norm1,
        lax.dynamic_slice_in_dim(y2, at, rows, 0),
        lax.dynamic_slice_in_dim(image, at, rows, 0),
        diag[:, None],
    )


def solution(mesh):
    n, cols = mesh.shape["blk"], mesh.shape["col"]
    placed = (
        P("blk", "col", None),
        P(("blk", "col"), None),
        P(("blk", "col"), None),
        P(("blk", "col")),
    )

    cubes = cols == 1 and n >= 16 and n & (n - 1) == 0

    def per_device(kernel, ritz_block, search_block, precond_diag):
        rows = kernel[:, 0, :]
        if cubes:
            return cubed(n, rows, ritz_block, search_block, precond_diag)
        return general(n, cols, rows, ritz_block, search_block, precond_diag)

    return jax.shard_map(
        per_device,
        mesh=mesh,
        in_specs=placed,
        out_specs=(P(("blk", "col"), None), P(("blk", "col"), None), P()),
        check_vma=False,
    )
```

```python
import jax
import jax.numpy as jnp
from jax import lax
from jax.experimental import pallas as pl
from jax.experimental.pallas import tpu as pltpu
from jax.sharding import PartitionSpec as P


ITERS = 2
F32 = jnp.float32
BF16 = jnp.bfloat16
highest = lax.Precision.HIGHEST
CHUNK = 512


def params(mebibytes=56):
    return pltpu.CompilerParams(vmem_limit_bytes=mebibytes << 20)


def mm(a, b, ca=1, cb=0):
    return lax.dot_general(
        a, b, (((ca,), (cb,)), ((), ())), precision=highest, preferred_element_type=F32
    )


def halves(x):
    top = x.astype(BF16)
    return top, (x - top.astype(F32)).astype(BF16)


def stacked(b, cb=0):
    b1, b2 = halves(b)
    return jnp.concatenate([b1, b2, b1], cb)


def mm3(a, b, ca=1, cb=0):
    return with_stacked(a, stacked(b, cb), ca, cb)


def with_stacked(a, b3, ca=1, cb=0):
    a1, a2 = halves(a)
    return lax.dot_general(
        jnp.concatenate([a1, a1, a2], ca),
        b3,
        (((ca,), (cb,)), ((), ())),
        preferred_element_type=F32,
    )


def pair_sum(terms):
    terms = list(terms)
    while len(terms) > 1:
        terms = [sum(terms[i + 1 : i + 2], terms[i]) for i in range(0, len(terms), 2)]
    return terms[0]


def total_of(xs, ys):
    return pair_sum(x * y for x, y in zip(xs, ys))


def solved(entry, columns, leaf):
    size = len(columns[0])
    if size == 2:
        x, y, z = entry(0, 0), entry(0, 1), entry(1, 1)
        scale = 1.0 / (x * z - y * y)
        q00, q01, q11 = z * scale, -(y * scale), x * scale
        leaf(x, y, z, columns[-1])
        return [[q00 * c[0] + q01 * c[1], q01 * c[0] + q11 * c[1]] for c in columns]
    h = size // 2
    side = [[entry(i, h + j) for i in range(h)] for j in range(h)]
    done = solved(entry, side + [c[:h] for c in columns], leaf)
    ties, upper = done[:h], done[h:]
    rest = {
        (i, j): entry(h + i, h + j) - total_of(side[i], ties[j])
        for j in range(h)
        for i in range(j + 1)
    }
    lower = solved(
        lambda i, j: rest[i, j],
        [[c[h + j] - total_of(ties[j], c[:h]) for j in range(h)] for c in columns],
        leaf,
    )
    return [
        [u[i] - total_of([ties[j][i] for j in range(h)], g) for i in range(h)] + g
        for u, g in zip(upper, lower)
    ]


def inverse_factor(matrix, panel=32):
    n, step = matrix.shape[0], 8
    lane = lax.broadcasted_iota(jnp.int32, (8, n), 1)
    sub = lax.broadcasted_iota(jnp.int32, (8, n), 0)
    a = [matrix[8 * v : 8 * v + 8, :] for v in range(n // 8)]
    zero = a[0] * 0.0

    def along(x, j):
        return jnp.broadcast_to(x[:, j : j + 1], (8, n))

    def down(x, i):
        return jnp.broadcast_to(x[i : i + 1, :], (8, n))

    rows = []
    for first in range(0, n, panel):
        last = (first + panel) // 8
        multipliers = []
        for k in range(first, first + panel, step):
            r = k // 8
            own = [along(a[r], k + j) + zero for j in range(step)]
            pivot = {(i, j): down(own[j], i) for j in range(step) for i in range(j + 1)}
            inside = (lane >= k) & (lane < k + step)
            base = jnp.where(inside, jnp.where(lane - k == sub, 1.0, 0.0), a[r])
            finished = []

            def leaf(x, y, z, e):
                scale = lax.rsqrt(x)
                ratio = y * (scale * scale)
                finished.append(e[0] * scale)
                finished.append((e[1] - ratio * e[0]) * lax.rsqrt(z - y * ratio))

            g = solved(lambda i, j: pivot[i, j], [[down(base, i) for i in range(step)]], leaf)[0]
            row, held = finished[0], g[0]
            for i in range(1, step):
                row = jnp.where(sub == i, finished[i], row)
                held = jnp.where(sub == i, g[i], held)
            rows.append(jnp.where(lane <= sub + k, row, 0.0))
            multipliers.append(
                jnp.where((lane >= k + step) & (lane < first + panel), 0.0, held)
            )
            for v in range(r + 1, last):
                other = [along(a[v], k + j) for j in range(step)]
                a[v] = jnp.where(inside, 0.0, a[v]) - total_of(other, g)
        if last < n // 8:
            change = mm(
                jnp.concatenate(a[first // 8 : last], 0), jnp.concatenate(multipliers, 0), 0, 0
            )
            inside = (lane >= first) & (lane < first + panel)
            for v in range(last, n // 8):
                a[v] = jnp.where(inside, 0.0, a[v]) - change[8 * v : 8 * v + 8]
    return jnp.concatenate(rows, 0)


def layout_of(rings, early):
    column = [8 * z for z in range(rings)]
    if early:
        first = [[0, 2, 4, 6], column[1:]]
        column = column[1:]
    else:
        first = [column]
    chips = first + [[d ^ m for d in column] for m in (2, 4, 6)]
    return chips + [[d ^ 1 for d in piece] for piece in chips]


def pack_blocks(*refs):
    parts, out_ref = refs[:-1], refs[-1]
    at = 0
    for part in parts:
        out_ref[at : at + part.shape[0], :] = part[...]
        at += part.shape[0]


def join_blocks(a_ref, b_ref, out_ref, sems):
    rows = a_ref.shape[0]
    copies = [
        pltpu.make_async_copy(a_ref, out_ref.at[:rows, :], sems.at[0]),
        pltpu.make_async_copy(b_ref, out_ref.at[rows:, :], sems.at[1]),
    ]
    for copy in copies:
        copy.start()
    for copy in copies:
        copy.wait()


def joined(a, b):
    return pl.pallas_call(
        join_blocks,
        out_shape=shape(2 * a.shape[0], a.shape[1]),
        in_specs=[pl.BlockSpec(memory_space=pltpu.HBM)] * 2,
        out_specs=VMEM,
        scratch_shapes=[pltpu.SemaphoreType.DMA((2,))],
        compiler_params=params(2),
        cost_estimate=cost(1),
        name="own",
    )(a, b)


def packed(parts):
    rows = sum(part.shape[0] for part in parts)
    return pl.pallas_call(
        pack_blocks,
        out_shape=shape(rows, parts[0].shape[1]),
        in_specs=[VMEM] * len(parts),
        out_specs=VMEM,
        compiler_params=params(2),
        cost_estimate=cost(0.5),
    )(*parts)


def gather(block, n, early):
    def swap(x, m):
        return lax.ppermute(x, "blk", [(i, i ^ m) for i in range(n)])

    column = [swap(block, 8 * z) for z in range(1, n // 8)]
    if early:
        near = packed([block] + [swap(block, 2 * k) for k in (1, 2, 3)])
        column = packed(column)
        chips = [near, column]
    else:
        column = packed([block] + column)
        chips = [column]
    chips += [swap(column, 2 * k) for k in (1, 2, 3)]
    return chips + [swap(x, 1) for x in chips]


def assemble(me, pieces, rings, early, place):
    for piece, distances in zip(pieces, layout_of(rings, early)):
        for slot, distance in enumerate(distances):
            place(piece, slot, jnp.bitwise_xor(me, distance))


def first_product(rings, rows, me_ref, kernel_ref, diag_ref, *refs):
    pieces, (y_ref, ky_ref) = refs[:-2], refs[-2:]
    width = y_ref.shape[1] // 2

    def place(piece, slot, device):
        base = slot * 2 * rows
        at = pl.ds(pl.multiple_of(device * rows, rows), rows)
        y_ref[at, :width] = piece[base : base + rows, :]
        y_ref[at, width:] = piece[base + rows : base + 2 * rows, :]

    assemble(me_ref[0], pieces, rings, True, place)
    result = mm3(kernel_ref[...], y_ref[...])
    ky_ref[:rows, :] = result[:, :width]
    ky_ref[rows : 2 * rows, :] = result[:, width:]
    ky_ref[2 * rows :, :] = jnp.zeros((8, width), F32)
    ky_ref[2 * rows : 2 * rows + 1, :rows] = diag_ref[...]


def metric_head(y_ref, metric_ref, upper_ref):
    total, double = y_ref.shape
    width = double // 2
    chunk = min(CHUNK, total)

    def add(i, acc):
        top, rest = halves(y_ref[pl.ds(pl.multiple_of(i * chunk, chunk), chunk), :])
        product = lax.dot_general(
            top,
            jnp.concatenate([top, rest], 1),
            (((0,), (0,)), ((), ())),
            preferred_element_type=F32,
        )
        return acc + product

    sums = lax.fori_loop(0, total // chunk, add, jnp.zeros((double, 2 * double), F32))
    metric = sums[:, :double] + (sums[:, double:] + sums[:, double:].T)
    metric_ref[...] = metric
    upper_ref[...] = inverse_factor(metric[:width, :width])


def metric_tail(metric_ref, upper_ref, out_ref):
    width = upper_ref.shape[0]
    upper = upper_ref[...]
    cross = mm(upper, metric_ref[:width, width:])
    lower = inverse_factor(metric_ref[width:, width:] - mm(cross, cross, 0, 0))
    out_ref[:width, :width] = upper
    out_ref[:width, width:] = jnp.zeros((width, width), F32)
    out_ref[width:, :width] = -mm(lower, mm(cross, upper, 0, 0))
    out_ref[width:, width:] = lower


def divided(residual, diag, values):
    eye = lax.broadcasted_iota(jnp.int32, values.shape, 0) == lax.broadcasted_iota(
        jnp.int32, values.shape, 1
    )
    level = jnp.sum(jnp.where(eye, values, 0.0), axis=0, keepdims=True)
    return residual / jnp.maximum(jnp.abs(diag - level), 1.0)


def first_step(y_ref, ky_ref, factor_ref, diag_ref, y2_ref, kx_ref, small_ref, norm_ref):
    total, double = y_ref.shape
    width = double // 2
    rows = diag_ref.shape[0]
    chunk = min(CHUNK, total)

    def add(i, acc):
        at = pl.ds(pl.multiple_of(i * chunk, chunk), chunk)
        return acc + mm3(y_ref[at, :], ky_ref[at, :], 0, 0)

    g = lax.fori_loop(0, total // chunk, add, jnp.zeros((double, double), F32))
    factor = factor_ref[...]
    tie = g[:width, width:].T
    side = jnp.concatenate([g[:width, :width], tie], 0)
    whole = jnp.concatenate([g[:width, :], jnp.concatenate([tie, g[width:, width:]], 1)], 0)
    z = mm3(factor, side)
    small = inverse_factor(mm3(z, z, 0, 0))
    raw = mm3(factor, z, 0, 0)
    held = mm3(jnp.concatenate([raw, mm3(whole, raw)], 0), small, 1, 1)
    mixing = held[:double]
    values = mm3(mixing, held[double:], 0, 0)
    both = stacked(jnp.concatenate([mixing, mm3(mixing, values)], 1))
    mixing = stacked(mixing)
    small_ref[...] = values

    def update(i, acc):
        at = pl.ds(pl.multiple_of(i * chunk, chunk), chunk)
        pair = with_stacked(y_ref[at, :], both)
        image = with_stacked(ky_ref[at, :], mixing)
        y2_ref[at, :width] = pair[:, :width]
        kx_ref[at, :] = image
        residual = image - pair[:, width:]
        y2_ref[at, width:] = residual
        return acc + jnp.sum(residual * residual, axis=0, keepdims=True)

    squares = lax.fori_loop(0, total // chunk, update, jnp.zeros((1, width), F32))
    norm_ref[...] = jnp.sqrt(squares)
    for b in range(total // rows):
        at = pl.ds(b * rows, rows)
        y2_ref[at, width:] = divided(y2_ref[at, width:], diag_ref[:rows, b : b + 1], values)


def with_product(rings, rows, me_ref, kernel_ref, y_ref, factor_ref, *refs):
    pieces = refs[:-8]
    y2_ref, kx_ref, small_ref, norm_ref, kw_ref, ky_ref, table, diag_ref = refs[-8:]
    width = kx_ref.shape[1]
    step = 2 * rows + 8

    def place(piece, slot, device):
        base = slot * step
        at = pl.ds(pl.multiple_of(device * rows, rows), rows)
        ky_ref[at, :width] = piece[base : base + rows, :]
        ky_ref[at, width:] = piece[base + rows : base + 2 * rows, :]
        table[pl.ds(device, 1), :] = piece[base + 2 * rows : base + 2 * rows + 1, :]

    table[...] = jnp.zeros_like(table)
    assemble(me_ref[0], pieces, rings, True, place)
    diag_ref[...] = table[...].T
    first_step(
        y_ref, ky_ref, factor_ref, diag_ref.at[:rows, :], y2_ref, kx_ref, small_ref, norm_ref
    )
    kw_ref[...] = mm3(kernel_ref[...], y2_ref[:, width:])


def second_factor(y2_ref, small_ref, tie_ref, factor_ref, known_ref, square_ref):
    total, double = y2_ref.shape
    width = double // 2
    chunk = min(CHUNK, total)

    def add(i, acc):
        at = pl.ds(pl.multiple_of(i * chunk, chunk), chunk)
        return acc + mm3(y2_ref[at, width:], y2_ref[at, :], 0, 0)

    gram = lax.fori_loop(0, total // chunk, add, jnp.zeros((width, double), F32))
    tie = gram[:, :width]
    values = small_ref[...]
    factor = inverse_factor(gram[:, width:] - mm(tie, tie, 1, 1))
    tie_ref[...] = tie
    factor_ref[...] = factor
    known_ref[...] = mm(factor, mm(tie, values))
    square_ref[...] = mm(values, values, 0, 0)


def second_step(y2_ref, image_ref, known, first_ref, own_y2, own_image, own_diag, outs):
    ritz_ref, search_ref, norm_ref = outs
    total, double = y2_ref.shape
    width = double // 2
    chunk = min(CHUNK, total)

    def add(i, acc):
        at = pl.ds(pl.multiple_of(i * chunk, chunk), chunk)
        return acc + mm3(image_ref[at, width:], y2_ref[at, :], 0, 0)

    g = lax.fori_loop(0, total // chunk, add, jnp.zeros((width, double), F32))
    values, tie, factor, done, square = [ref[...] for ref in known]
    z = mm3(factor, g[:, :width]) - done
    small = inverse_factor(square + mm3(z, z, 0, 0))
    lower = mm3(factor, z, 0, 0)
    raw = jnp.concatenate([values - mm3(tie, lower, 0, 0), lower], 0)
    whole = jnp.concatenate([jnp.concatenate([values, g[:, :width].T], 1), g], 0)
    held = mm3(jnp.concatenate([raw, mm3(whole, raw)], 0), small, 1, 1)
    mixing = held[:double]
    values2 = mm3(mixing, held[double:], 0, 0)
    weights = stacked(jnp.concatenate([mixing, -mm3(mixing, values2)], 0))

    def update(i, acc):
        at = pl.ds(pl.multiple_of(i * chunk, chunk), chunk)
        residual = with_stacked(jnp.concatenate([image_ref[at, :], y2_ref[at, :]], 1), weights)
        return acc + jnp.sum(residual * residual, axis=0, keepdims=True)

    squares = lax.fori_loop(0, total // chunk, update, jnp.zeros((1, width), F32))
    norm_ref[:1, :] = first_ref[...]
    norm_ref[1:, :] = jnp.sqrt(squares)
    own = own_y2()
    ritz_ref[...] = mm3(own, mixing)
    residual = with_stacked(jnp.concatenate([own_image(), own], 1), weights)
    search_ref[...] = divided(residual, own_diag(), values2)


def last_step(rings, rows, me_ref, y2_ref, kx_ref, first_ref, diag_ref, *refs):
    known, pieces = refs[:5], refs[5:-4]
    ritz_ref, search_ref, norm_ref, image_ref = refs[-4:]
    width = kx_ref.shape[1]
    me = me_ref[0]

    def place(piece, slot, device):
        at = pl.ds(pl.multiple_of(device * rows, rows), rows)
        image_ref[at, width:] = piece[slot * rows : (slot + 1) * rows, :]

    assemble(me, pieces, rings, False, place)
    image_ref[:, :width] = kx_ref[...]
    mine = pl.ds(pl.multiple_of(me * rows, rows), rows)
    second_step(
        y2_ref,
        image_ref,
        known,
        first_ref,
        lambda: y2_ref[mine, :],
        lambda: image_ref[mine, :],
        lambda: jnp.broadcast_to(diag_ref[...], (8, rows)).T[:, :1],
        (ritz_ref, search_ref, norm_ref),
    )


def general_last(y2_ref, image_ref, first_ref, own_y2, own_image, own_diag, *refs):
    known, outs = refs[:5], refs[5:]
    second_step(
        y2_ref,
        image_ref,
        known,
        first_ref,
        lambda: own_y2[...],
        lambda: own_image[...],
        lambda: own_diag[...],
        outs,
    )


def cost(us):
    return pl.CostEstimate(flops=int(us * 1e9), bytes_accessed=0, transcendentals=0)


def shape(*dims):
    return jax.ShapeDtypeStruct(dims, F32)


VMEM = pl.BlockSpec(memory_space=pltpu.VMEM)
SMEM = pl.BlockSpec(memory_space=pltpu.SMEM)


def metric_factor(y, mebibytes):
    width = y.shape[1] // 2
    metric, upper = pl.pallas_call(
        metric_head,
        out_shape=(shape(2 * width, 2 * width), shape(width, width)),
        in_specs=[VMEM],
        out_specs=(VMEM, VMEM),
        compiler_params=params(mebibytes),
        cost_estimate=cost(7),
        name="metric_head",
    )(y)
    return pl.pallas_call(
        metric_tail,
        out_shape=shape(2 * width, 2 * width),
        in_specs=[VMEM, VMEM],
        out_specs=VMEM,
        compiler_params=params(mebibytes),
        cost_estimate=cost(7),
        name="metric_tail",
    )(metric, upper)


def second_metric(y2, values, mebibytes):
    width = y2.shape[1] // 2
    return pl.pallas_call(
        second_factor,
        out_shape=(shape(width, width),) * 4,
        in_specs=[VMEM] * 2,
        out_specs=(VMEM,) * 4,
        compiler_params=params(mebibytes),
        cost_estimate=cost(9),
        name="second_factor",
    )(y2, values)


def cubed(n, kernel, ritz, search, diag):
    rows, width = ritz.shape
    rings = n // 8
    total = n * rows
    lanes = max(n, 128)
    me = lax.axis_index("blk").astype(jnp.int32).reshape(1)
    along = diag.reshape(1, rows)
    sent = gather(joined(ritz, search), n, True)
    y, ky_own = pl.pallas_call(
        lambda *refs: first_product(rings, rows, *refs),
        out_shape=(shape(total, 2 * width), shape(2 * rows + 8, width)),
        in_specs=[SMEM, VMEM, VMEM] + [VMEM] * len(sent),
        out_specs=(VMEM, VMEM),
        compiler_params=params(16),
        name="first_product",
    )(me, kernel, along, *sent)
    images = gather(ky_own, n, True)
    factor = metric_factor(y, 12)
    y2, kx, values, norm1, kw_own = pl.pallas_call(
        lambda *refs: with_product(rings, rows, *refs),
        out_shape=(
            shape(total, 2 * width),
            shape(total, width),
            shape(width, width),
            shape(1, width),
            shape(rows, width),
        ),
        in_specs=[SMEM] + [VMEM] * (3 + len(images)),
        out_specs=(VMEM,) * 5,
        scratch_shapes=[
            pltpu.VMEM((total, 2 * width), F32),
            pltpu.VMEM((lanes, width), F32),
            pltpu.VMEM((width, lanes), F32),
        ],
        compiler_params=params(24),
        name="first_step",
    )(me, kernel, y, factor, *images)
    images2 = gather(kw_own, n, False)
    known = second_metric(y2, values, 12)
    return pl.pallas_call(
        lambda *refs: last_step(rings, rows, *refs),
        out_shape=(shape(rows, width), shape(rows, width), shape(ITERS, width)),
        in_specs=[SMEM] + [VMEM] * (9 + len(images2)),
        out_specs=(VMEM,) * 3,
        scratch_shapes=[pltpu.VMEM((total, 2 * width), F32)],
        compiler_params=params(24),
        name="last_step",
    )(me, y2, kx, norm1, along, values, *known, *images2)


def general(n, cols, kernel, ritz, search, diag):
    rows, width = ritz.shape
    axes = ("blk", "col")
    total = n * cols * rows
    q = lax.axis_index("col")

    def product(part):
        whole = lax.psum_scatter(mm(kernel, part), "col", scatter_dimension=0, tiled=True)
        return whole

    own = jnp.concatenate([ritz, search], 1)
    part = lax.all_gather(own, "blk", axis=0, tiled=True)
    y = lax.all_gather(own, axes, axis=0, tiled=True)
    ky = lax.all_gather(product(part), axes, axis=0, tiled=True)
    table = lax.all_gather(diag, axes, axis=0, tiled=True).reshape(n * cols, rows).T
    factor = metric_factor(y, 56)
    y2, kx, values, norm1 = pl.pallas_call(
        first_step,
        out_shape=(shape(total, 2 * width), shape(total, width), shape(width, width), shape(1, width)),
        in_specs=[VMEM] * 4,
        out_specs=(VMEM,) * 4,
        compiler_params=params(),
        name="first_step",
    )(y, ky, factor, table)
    held = y2[:, width:].reshape(n, cols, rows, width)
    part2 = lax.dynamic_index_in_dim(held, q, 1, keepdims=False).reshape(n * rows, width)
    kw = lax.all_gather(product(part2), axes, axis=0, tiled=True)
    known = second_metric(y2, values, 56)
    image = jnp.concatenate([kx, kw], 1)
    at = (lax.axis_index("blk") * cols + q) * rows
    return pl.pallas_call(
        general_last,
        out_shape=(shape(rows, width), shape(rows, width), shape(ITERS, width)),
        in_specs=[VMEM] * 11,
        out_specs=(VMEM,) * 3,
        compiler_params=params(),
        name="last_step",
    )(
        y2,
        image,
        norm1,
        lax.dynamic_slice_in_dim(y2, at, rows, 0),
        lax.dynamic_slice_in_dim(image, at, rows, 0),
        diag[:, None],
        values,
        *known,
    )


def solution(mesh):
    n, cols = mesh.shape["blk"], mesh.shape["col"]
    placed = (
        P("blk", "col", None),
        P(("blk", "col"), None),
        P(("blk", "col"), None),
        P(("blk", "col")),
    )

    cubes = cols == 1 and n >= 16 and n & (n - 1) == 0

    def per_device(kernel, ritz_block, search_block, precond_diag):
        rows = kernel[:, 0, :]
        if cubes:
            return cubed(n, rows, ritz_block, search_block, precond_diag)
        return general(n, cols, rows, ritz_block, search_block, precond_diag)

    return jax.shard_map(
        per_device,
        mesh=mesh,
        in_specs=placed,
        out_specs=(P(("blk", "col"), None), P(("blk", "col"), None), P()),
        check_vma=False,
    )
```

```python
import jax
import jax.numpy as jnp
from jax import lax
from jax.experimental import pallas as pl
from jax.experimental.pallas import tpu as pltpu
from jax.sharding import PartitionSpec as P


ITERS = 2
F32 = jnp.float32
BF16 = jnp.bfloat16
highest = lax.Precision.HIGHEST
CHUNK = 2048


def params(mebibytes=56):
    return pltpu.CompilerParams(vmem_limit_bytes=mebibytes << 20)


def mm(a, b, ca=1, cb=0):
    return lax.dot_general(
        a, b, (((ca,), (cb,)), ((), ())), precision=highest, preferred_element_type=F32
    )


def sweep(total, add, zero, chunk=CHUNK):
    chunk = min(chunk, total)
    if chunk == total:
        return add(pl.ds(0, total), zero)

    def part(i, acc):
        return add(pl.ds(pl.multiple_of(i * chunk, chunk), chunk), acc)

    return lax.fori_loop(0, total // chunk, part, zero)


def halves(x):
    top = x.astype(BF16)
    return top, (x - top.astype(F32)).astype(BF16)


def stacked(b, cb=0):
    b1, b2 = halves(b)
    return jnp.concatenate([b1, b2, b1], cb)


def mm3(a, b, ca=1, cb=0):
    return with_stacked(a, stacked(b, cb), ca, cb)


def with_stacked(a, b3, ca=1, cb=0):
    a1, a2 = halves(a)
    return lax.dot_general(
        jnp.concatenate([a1, a1, a2], ca),
        b3,
        (((ca,), (cb,)), ((), ())),
        preferred_element_type=F32,
    )


def pair_sum(terms):
    terms = list(terms)
    while len(terms) > 1:
        terms = [sum(terms[i + 1 : i + 2], terms[i]) for i in range(0, len(terms), 2)]
    return terms[0]


def total_of(xs, ys):
    return pair_sum(x * y for x, y in zip(xs, ys))


def solved(entry, columns, leaf):
    size = len(columns[0])
    if size == 2:
        x, y, z = entry(0, 0), entry(0, 1), entry(1, 1)
        scale = 1.0 / (x * z - y * y)
        q00, q01, q11 = z * scale, -(y * scale), x * scale
        leaf(x, y, z, columns[-1])
        return [[q00 * c[0] + q01 * c[1], q01 * c[0] + q11 * c[1]] for c in columns]
    h = size // 2
    side = [[entry(i, h + j) for i in range(h)] for j in range(h)]
    done = solved(entry, side + [c[:h] for c in columns], leaf)
    ties, upper = done[:h], done[h:]
    rest = {
        (i, j): entry(h + i, h + j) - total_of(side[i], ties[j])
        for j in range(h)
        for i in range(j + 1)
    }
    lower = solved(
        lambda i, j: rest[i, j],
        [[c[h + j] - total_of(ties[j], c[:h]) for j in range(h)] for c in columns],
        leaf,
    )
    return [
        [u[i] - total_of([ties[j][i] for j in range(h)], g) for i in range(h)] + g
        for u, g in zip(upper, lower)
    ]


def inverse_factor(matrix, panel=32):
    n, step = matrix.shape[0], 8
    lane = lax.broadcasted_iota(jnp.int32, (8, n), 1)
    sub = lax.broadcasted_iota(jnp.int32, (8, n), 0)
    a = [matrix[8 * v : 8 * v + 8, :] for v in range(n // 8)]
    zero = a[0] * 0.0

    def along(x, j):
        return jnp.broadcast_to(x[:, j : j + 1], (8, n))

    def down(x, i):
        return jnp.broadcast_to(x[i : i + 1, :], (8, n))

    rows = []
    for first in range(0, n, panel):
        last = (first + panel) // 8
        multipliers = []
        for k in range(first, first + panel, step):
            r = k // 8
            own = [along(a[r], k + j) + zero for j in range(step)]
            pivot = {(i, j): down(own[j], i) for j in range(step) for i in range(j + 1)}
            inside = (lane >= k) & (lane < k + step)
            base = jnp.where(inside, jnp.where(lane - k == sub, 1.0, 0.0), a[r])
            finished = []

            def leaf(x, y, z, e):
                scale = lax.rsqrt(x)
                ratio = y * (scale * scale)
                finished.append(e[0] * scale)
                finished.append((e[1] - ratio * e[0]) * lax.rsqrt(z - y * ratio))

            g = solved(lambda i, j: pivot[i, j], [[down(base, i) for i in range(step)]], leaf)[0]
            row, held = finished[0], g[0]
            for i in range(1, step):
                row = jnp.where(sub == i, finished[i], row)
                held = jnp.where(sub == i, g[i], held)
            rows.append(jnp.where(lane <= sub + k, row, 0.0))
            multipliers.append(
                jnp.where((lane >= k + step) & (lane < first + panel), 0.0, held)
            )
            for v in range(r + 1, last):
                other = [along(a[v], k + j) for j in range(step)]
                a[v] = jnp.where(inside, 0.0, a[v]) - total_of(other, g)
        if last < n // 8:
            change = mm(
                jnp.concatenate(a[first // 8 : last], 0), jnp.concatenate(multipliers, 0), 0, 0
            )
            inside = (lane >= first) & (lane < first + panel)
            for v in range(last, n // 8):
                a[v] = jnp.where(inside, 0.0, a[v]) - change[8 * v : 8 * v + 8]
    return jnp.concatenate(rows, 0)


def layout_of(rings, early):
    column = [8 * z for z in range(rings)]
    if early:
        first = [[0, 2, 4, 6], column[1:]]
        column = column[1:]
    else:
        first = [column]
    chips = first + [[d ^ m for d in column] for m in (2, 4, 6)]
    return chips + [[d ^ 1 for d in piece] for piece in chips]


def pack_blocks(*refs):
    parts, out_ref = refs[:-1], refs[-1]
    at = 0
    for part in parts:
        out_ref[at : at + part.shape[0], :] = part[...]
        at += part.shape[0]


def packed(parts):
    rows = sum(part.shape[0] for part in parts)
    return pl.pallas_call(
        pack_blocks,
        out_shape=shape(rows, parts[0].shape[1]),
        in_specs=[VMEM] * len(parts),
        out_specs=VMEM,
        compiler_params=params(2),
        cost_estimate=cost(0.5),
    )(*parts)


def gather(block, n, early):
    def swap(x, m):
        return lax.ppermute(x, "blk", [(i, i ^ m) for i in range(n)])

    column = [swap(block, 8 * z) for z in range(1, n // 8)]
    if early:
        near = packed([block] + [swap(block, 2 * k) for k in (1, 2, 3)])
        column = packed(column)
        chips = [near, column]
    else:
        column = packed([block] + column)
        chips = [column]
    chips += [swap(column, 2 * k) for k in (1, 2, 3)]
    return chips + [swap(x, 1) for x in chips]


def assemble(me, pieces, rings, early, place):
    for piece, distances in zip(pieces, layout_of(rings, early)):
        for slot, distance in enumerate(distances):
            place(piece, slot, jnp.bitwise_xor(me, distance))


def first_product(rings, rows, me_ref, kernel_ref, diag_ref, *refs):
    pieces, (y_ref, ky_ref) = refs[:-2], refs[-2:]
    width = y_ref.shape[1] // 2

    def place(piece, slot, device):
        base = slot * 2 * rows
        at = pl.ds(pl.multiple_of(device * rows, rows), rows)
        y_ref[at, :width] = piece[base : base + rows, :]
        y_ref[at, width:] = piece[base + rows : base + 2 * rows, :]

    assemble(me_ref[0], pieces, rings, True, place)
    result = mm3(kernel_ref[...], y_ref[...])
    ky_ref[:rows, :] = result[:, :width]
    ky_ref[rows : 2 * rows, :] = result[:, width:]
    ky_ref[2 * rows :, :] = jnp.zeros((8, width), F32)
    ky_ref[2 * rows : 2 * rows + 1, :rows] = diag_ref[...]


def metric_kernel(y_ref, out_ref):
    total, double = y_ref.shape
    width = double // 2

    def add(at, acc):
        top, rest = halves(y_ref[at, :])
        product = lax.dot_general(
            top,
            jnp.concatenate([top, rest], 1),
            (((0,), (0,)), ((), ())),
            preferred_element_type=F32,
        )
        return acc + product

    sums = sweep(total, add, jnp.zeros((double, 2 * double), F32))
    metric = sums[:, :double] + (sums[:, double:] + sums[:, double:].T)
    upper = inverse_factor(metric[:width, :width])
    cross = mm(upper, metric[:width, width:])
    lower = inverse_factor(metric[width:, width:] - mm(cross, cross, 0, 0))
    out_ref[:width, :width] = upper
    out_ref[:width, width:] = jnp.zeros((width, width), F32)
    out_ref[width:, :width] = -mm(lower, mm(cross, upper, 0, 0))
    out_ref[width:, width:] = lower


def divided(residual, diag, values):
    eye = lax.broadcasted_iota(jnp.int32, values.shape, 0) == lax.broadcasted_iota(
        jnp.int32, values.shape, 1
    )
    level = jnp.sum(jnp.where(eye, values, 0.0), axis=0, keepdims=True)
    return residual / jnp.maximum(jnp.abs(diag - level), 1.0)


def first_step(y_ref, ky_ref, factor_ref, diag_ref, y2_ref, kx_ref, small_ref, norm_ref):
    total, double = y_ref.shape
    width = double // 2
    rows = diag_ref.shape[0]

    def add(at, acc):
        return acc + mm3(y_ref[at, :], ky_ref[at, :], 0, 0)

    g = sweep(total, add, jnp.zeros((double, double), F32), 1024)
    factor = factor_ref[...]
    tie = g[:width, width:].T
    side = jnp.concatenate([g[:width, :width], tie], 0)
    whole = jnp.concatenate([g[:width, :], jnp.concatenate([tie, g[width:, width:]], 1)], 0)
    z = mm3(factor, side)
    small = inverse_factor(mm3(z, z, 0, 0))
    raw = mm3(factor, z, 0, 0)
    held = mm3(jnp.concatenate([raw, mm3(whole, raw)], 0), small, 1, 1)
    mixing = held[:double]
    values = mm3(mixing, held[double:], 0, 0)
    both = stacked(jnp.concatenate([mixing, mm3(mixing, values)], 1))
    mixing = stacked(mixing)
    small_ref[...] = values

    def update(at, acc):
        pair = with_stacked(y_ref[at, :], both)
        image = with_stacked(ky_ref[at, :], mixing)
        y2_ref[at, :width] = pair[:, :width]
        kx_ref[at, :] = image
        residual = image - pair[:, width:]
        y2_ref[at, width:] = residual
        return acc + jnp.sum(residual * residual, axis=0, keepdims=True)

    squares = sweep(total, update, jnp.zeros((1, width), F32))
    norm_ref[...] = jnp.sqrt(squares)
    for b in range(total // rows):
        at = pl.ds(b * rows, rows)
        y2_ref[at, width:] = divided(y2_ref[at, width:], diag_ref[:rows, b : b + 1], values)


def with_product(rings, rows, me_ref, kernel_ref, y_ref, factor_ref, *refs):
    pieces = refs[:-8]
    y2_ref, kx_ref, small_ref, norm_ref, kw_ref, ky_ref, table, diag_ref = refs[-8:]
    width = kx_ref.shape[1]
    step = 2 * rows + 8

    def place(piece, slot, device):
        base = slot * step
        at = pl.ds(pl.multiple_of(device * rows, rows), rows)
        ky_ref[at, :width] = piece[base : base + rows, :]
        ky_ref[at, width:] = piece[base + rows : base + 2 * rows, :]
        table[pl.ds(device, 1), :] = piece[base + 2 * rows : base + 2 * rows + 1, :]

    table[...] = jnp.zeros_like(table)
    assemble(me_ref[0], pieces, rings, True, place)
    diag_ref[...] = table[...].T
    first_step(
        y_ref, ky_ref, factor_ref, diag_ref.at[:rows, :], y2_ref, kx_ref, small_ref, norm_ref
    )
    kw_ref[...] = mm3(kernel_ref[...], y2_ref[:, width:])


def second_factor(y2_ref, small_ref, tie_ref, factor_ref, known_ref, square_ref):
    total, double = y2_ref.shape
    width = double // 2

    def add(at, acc):
        return acc + mm3(y2_ref[at, width:], y2_ref[at, :], 0, 0)

    gram = sweep(total, add, jnp.zeros((width, double), F32))
    tie = gram[:, :width]
    values = small_ref[...]
    factor = inverse_factor(gram[:, width:] - mm(tie, tie, 1, 1))
    tie_ref[...] = tie
    factor_ref[...] = factor
    known_ref[...] = mm(factor, mm(tie, values))
    square_ref[...] = mm(values, values, 0, 0)


def second_step(y2_ref, image_ref, known, first_ref, own_y2, own_image, own_diag, outs):
    ritz_ref, search_ref, norm_ref = outs
    total, double = y2_ref.shape
    width = double // 2

    def add(at, acc):
        return acc + mm3(image_ref[at, width:], y2_ref[at, :], 0, 0)

    g = sweep(total, add, jnp.zeros((width, double), F32))
    values, tie, factor, done, square = [ref[...] for ref in known]
    z = mm3(factor, g[:, :width]) - done
    small = inverse_factor(square + mm3(z, z, 0, 0))
    lower = mm3(factor, z, 0, 0)
    raw = jnp.concatenate([values - mm3(tie, lower, 0, 0), lower], 0)
    whole = jnp.concatenate([jnp.concatenate([values, g[:, :width].T], 1), g], 0)
    held = mm3(jnp.concatenate([raw, mm3(whole, raw)], 0), small, 1, 1)
    mixing = held[:double]
    values2 = mm3(mixing, held[double:], 0, 0)
    weights = stacked(jnp.concatenate([mixing, -mm3(mixing, values2)], 0))

    def update(at, acc):
        residual = with_stacked(jnp.concatenate([image_ref[at, :], y2_ref[at, :]], 1), weights)
        return acc + jnp.sum(residual * residual, axis=0, keepdims=True)

    squares = sweep(total, update, jnp.zeros((1, width), F32))
    norm_ref[:1, :] = first_ref[...]
    norm_ref[1:, :] = jnp.sqrt(squares)
    own = own_y2()
    ritz_ref[...] = mm3(own, mixing)
    residual = with_stacked(jnp.concatenate([own_image(), own], 1), weights)
    search_ref[...] = divided(residual, own_diag(), values2)


def last_step(rings, rows, me_ref, y2_ref, kx_ref, first_ref, diag_ref, *refs):
    known, pieces = refs[:5], refs[5:-4]
    ritz_ref, search_ref, norm_ref, image_ref = refs[-4:]
    width = kx_ref.shape[1]
    me = me_ref[0]

    def place(piece, slot, device):
        at = pl.ds(pl.multiple_of(device * rows, rows), rows)
        image_ref[at, width:] = piece[slot * rows : (slot + 1) * rows, :]

    assemble(me, pieces, rings, False, place)
    image_ref[:, :width] = kx_ref[...]
    mine = pl.ds(pl.multiple_of(me * rows, rows), rows)
    second_step(
        y2_ref,
        image_ref,
        known,
        first_ref,
        lambda: y2_ref[mine, :],
        lambda: image_ref[mine, :],
        lambda: jnp.broadcast_to(diag_ref[...], (8, rows)).T[:, :1],
        (ritz_ref, search_ref, norm_ref),
    )


def general_last(y2_ref, image_ref, first_ref, own_y2, own_image, own_diag, *refs):
    known, outs = refs[:5], refs[5:]
    second_step(
        y2_ref,
        image_ref,
        known,
        first_ref,
        lambda: own_y2[...],
        lambda: own_image[...],
        lambda: own_diag[...],
        outs,
    )


def cost(us):
    return pl.CostEstimate(flops=int(us * 1e9), bytes_accessed=0, transcendentals=0)


def shape(*dims):
    return jax.ShapeDtypeStruct(dims, F32)


VMEM = pl.BlockSpec(memory_space=pltpu.VMEM)
SMEM = pl.BlockSpec(memory_space=pltpu.SMEM)


def metric_factor(y, mebibytes):
    double = y.shape[1]
    return pl.pallas_call(
        metric_kernel,
        out_shape=shape(double, double),
        in_specs=[VMEM],
        out_specs=VMEM,
        compiler_params=params(mebibytes),
        cost_estimate=cost(9),
        name="metric",
    )(y)


def second_metric(y2, values, mebibytes):
    width = y2.shape[1] // 2
    return pl.pallas_call(
        second_factor,
        out_shape=(shape(width, width),) * 4,
        in_specs=[VMEM] * 2,
        out_specs=(VMEM,) * 4,
        compiler_params=params(mebibytes),
        cost_estimate=cost(9),
        name="second_factor",
    )(y2, values)


def cubed(n, kernel, ritz, search, diag):
    rows, width = ritz.shape
    rings = n // 8
    total = n * rows
    lanes = max(n, 128)
    me = lax.axis_index("blk").astype(jnp.int32).reshape(1)
    along = diag.reshape(1, rows)
    own = lax.pad(ritz, 0.0, ((0, rows, 0), (0, 0, 0))) + lax.pad(search, 0.0, ((rows, 0, 0), (0, 0, 0)))
    sent = gather(own, n, True)
    y, ky_own = pl.pallas_call(
        lambda *refs: first_product(rings, rows, *refs),
        out_shape=(shape(total, 2 * width), shape(2 * rows + 8, width)),
        in_specs=[SMEM, VMEM, VMEM] + [VMEM] * len(sent),
        out_specs=(VMEM, VMEM),
        compiler_params=params(16),
        name="first_product",
    )(me, kernel, along, *sent)
    images = gather(ky_own, n, True)
    factor = metric_factor(y, 12)
    y2, kx, values, norm1, kw_own = pl.pallas_call(
        lambda *refs: with_product(rings, rows, *refs),
        out_shape=(
            shape(total, 2 * width),
            shape(total, width),
            shape(width, width),
            shape(1, width),
            shape(rows, width),
        ),
        in_specs=[SMEM] + [VMEM] * (3 + len(images)),
        out_specs=(VMEM,) * 5,
        scratch_shapes=[
            pltpu.VMEM((total, 2 * width), F32),
            pltpu.VMEM((lanes, width), F32),
            pltpu.VMEM((width, lanes), F32),
        ],
        compiler_params=params(24),
        name="first_step",
    )(me, kernel, y, factor, *images)
    images2 = gather(kw_own, n, False)
    known = second_metric(y2, values, 12)
    return pl.pallas_call(
        lambda *refs: last_step(rings, rows, *refs),
        out_shape=(shape(rows, width), shape(rows, width), shape(ITERS, width)),
        in_specs=[SMEM] + [VMEM] * (9 + len(images2)),
        out_specs=(VMEM,) * 3,
        scratch_shapes=[pltpu.VMEM((total, 2 * width), F32)],
        compiler_params=params(24),
        name="last_step",
    )(me, y2, kx, norm1, along, values, *known, *images2)


def general(n, cols, kernel, ritz, search, diag):
    rows, width = ritz.shape
    axes = ("blk", "col")
    total = n * cols * rows
    q = lax.axis_index("col")

    def product(part):
        whole = lax.psum_scatter(mm(kernel, part), "col", scatter_dimension=0, tiled=True)
        return whole

    own = jnp.concatenate([ritz, search], 1)
    part = lax.all_gather(own, "blk", axis=0, tiled=True)
    y = lax.all_gather(own, axes, axis=0, tiled=True)
    ky = lax.all_gather(product(part), axes, axis=0, tiled=True)
    table = lax.all_gather(diag, axes, axis=0, tiled=True).reshape(n * cols, rows).T
    factor = metric_factor(y, 56)
    y2, kx, values, norm1 = pl.pallas_call(
        first_step,
        out_shape=(shape(total, 2 * width), shape(total, width), shape(width, width), shape(1, width)),
        in_specs=[VMEM] * 4,
        out_specs=(VMEM,) * 4,
        compiler_params=params(),
        name="first_step",
    )(y, ky, factor, table)
    held = y2[:, width:].reshape(n, cols, rows, width)
    part2 = lax.dynamic_index_in_dim(held, q, 1, keepdims=False).reshape(n * rows, width)
    kw = lax.all_gather(product(part2), axes, axis=0, tiled=True)
    known = second_metric(y2, values, 56)
    image = jnp.concatenate([kx, kw], 1)
    at = (lax.axis_index("blk") * cols + q) * rows
    return pl.pallas_call(
        general_last,
        out_shape=(shape(rows, width), shape(rows, width), shape(ITERS, width)),
        in_specs=[VMEM] * 11,
        out_specs=(VMEM,) * 3,
        compiler_params=params(),
        name="last_step",
    )(
        y2,
        image,
        norm1,
        lax.dynamic_slice_in_dim(y2, at, rows, 0),
        lax.dynamic_slice_in_dim(image, at, rows, 0),
        diag[:, None],
        values,
        *known,
    )


def solution(mesh):
    n, cols = mesh.shape["blk"], mesh.shape["col"]
    placed = (
        P("blk", "col", None),
        P(("blk", "col"), None),
        P(("blk", "col"), None),
        P(("blk", "col")),
    )

    cubes = cols == 1 and n >= 16 and n & (n - 1) == 0

    def per_device(kernel, ritz_block, search_block, precond_diag):
        rows = kernel[:, 0, :]
        if cubes:
            return cubed(n, rows, ritz_block, search_block, precond_diag)
        return general(n, cols, rows, ritz_block, search_block, precond_diag)

    return jax.shard_map(
        per_device,
        mesh=mesh,
        in_specs=placed,
        out_specs=(P(("blk", "col"), None), P(("blk", "col"), None), P()),
        check_vma=False,
    )
```

```python
import jax
import jax.numpy as jnp
from jax import lax
from jax.experimental import pallas as pl
from jax.experimental.pallas import tpu as pltpu
from jax.sharding import PartitionSpec as P


ITERS = 2
F32 = jnp.float32
BF16 = jnp.bfloat16
highest = lax.Precision.HIGHEST
CHUNK = 2048
EARLY = ((1, 2, 3), (1, 2, 3), (1, 2, 3))


def params(mebibytes=56):
    return pltpu.CompilerParams(vmem_limit_bytes=mebibytes << 20)


def mm(a, b, ca=1, cb=0):
    return lax.dot_general(
        a, b, (((ca,), (cb,)), ((), ())), precision=highest, preferred_element_type=F32
    )


def sweep(total, add, zero, chunk=CHUNK):
    chunk = min(chunk, total)
    if chunk == total:
        return add(pl.ds(0, total), zero)

    def part(i, acc):
        return add(pl.ds(pl.multiple_of(i * chunk, chunk), chunk), acc)

    return lax.fori_loop(0, total // chunk, part, zero)


def halves(x):
    top = x.astype(BF16)
    return top, (x - top.astype(F32)).astype(BF16)


def stacked(b, cb=0):
    b1, b2 = halves(b)
    return jnp.concatenate([b1, b2, b1], cb)


def mm3(a, b, ca=1, cb=0):
    return with_stacked(a, stacked(b, cb), ca, cb)


def with_stacked(a, b3, ca=1, cb=0):
    a1, a2 = halves(a)
    return lax.dot_general(
        jnp.concatenate([a1, a1, a2], ca),
        b3,
        (((ca,), (cb,)), ((), ())),
        preferred_element_type=F32,
    )


def pair_sum(terms):
    terms = list(terms)
    while len(terms) > 1:
        terms = [sum(terms[i + 1 : i + 2], terms[i]) for i in range(0, len(terms), 2)]
    return terms[0]


def total_of(xs, ys):
    return pair_sum(x * y for x, y in zip(xs, ys))


def solved(entry, columns, leaf):
    size = len(columns[0])
    if size == 2:
        x, y, z = entry(0, 0), entry(0, 1), entry(1, 1)
        scale = 1.0 / (x * z - y * y)
        q00, q01, q11 = z * scale, -(y * scale), x * scale
        leaf(x, y, z, columns[-1])
        return [[q00 * c[0] + q01 * c[1], q01 * c[0] + q11 * c[1]] for c in columns]
    h = size // 2
    side = [[entry(i, h + j) for i in range(h)] for j in range(h)]
    done = solved(entry, side + [c[:h] for c in columns], leaf)
    ties, upper = done[:h], done[h:]
    rest = {
        (i, j): entry(h + i, h + j) - total_of(side[i], ties[j])
        for j in range(h)
        for i in range(j + 1)
    }
    lower = solved(
        lambda i, j: rest[i, j],
        [[c[h + j] - total_of(ties[j], c[:h]) for j in range(h)] for c in columns],
        leaf,
    )
    return [
        [u[i] - total_of([ties[j][i] for j in range(h)], g) for i in range(h)] + g
        for u, g in zip(upper, lower)
    ]


def inverse_factor(matrix, panel=128):
    n, step = matrix.shape[0], 8
    lane = lax.broadcasted_iota(jnp.int32, (8, n), 1)
    sub = lax.broadcasted_iota(jnp.int32, (8, n), 0)
    a = [matrix[8 * v : 8 * v + 8, :] for v in range(n // 8)]
    zero = a[0] * 0.0

    def along(x, j):
        return jnp.broadcast_to(x[:, j : j + 1], (8, n))

    def down(x, i):
        return jnp.broadcast_to(x[i : i + 1, :], (8, n))

    rows = []
    for first in range(0, n, panel):
        last = (first + panel) // 8
        multipliers = []
        for k in range(first, first + panel, step):
            r = k // 8
            own = [along(a[r], k + j) + zero for j in range(step)]
            pivot = {(i, j): down(own[j], i) for j in range(step) for i in range(j + 1)}
            inside = (lane >= k) & (lane < k + step)
            base = jnp.where(inside, jnp.where(lane - k == sub, 1.0, 0.0), a[r])
            finished = []

            def leaf(x, y, z, e):
                scale = lax.rsqrt(x)
                ratio = y * (scale * scale)
                finished.append(e[0] * scale)
                finished.append((e[1] - ratio * e[0]) * lax.rsqrt(z - y * ratio))

            g = solved(lambda i, j: pivot[i, j], [[down(base, i) for i in range(step)]], leaf)[0]
            row, held = finished[0], g[0]
            for i in range(1, step):
                row = jnp.where(sub == i, finished[i], row)
                held = jnp.where(sub == i, g[i], held)
            rows.append(jnp.where(lane <= sub + k, row, 0.0))
            multipliers.append(
                jnp.where((lane >= k + step) & (lane < first + panel), 0.0, held)
            )
            for v in range(r + 1, last):
                other = [along(a[v], k + j) for j in range(step)]
                a[v] = jnp.where(inside, 0.0, a[v]) - total_of(other, g)
        if last < n // 8:
            change = mm(
                jnp.concatenate(a[first // 8 : last], 0), jnp.concatenate(multipliers, 0), 0, 0
            )
            inside = (lane >= first) & (lane < first + panel)
            for v in range(last, n // 8):
                a[v] = jnp.where(inside, 0.0, a[v]) - change[8 * v : 8 * v + 8]
    return jnp.concatenate(rows, 0)


def layout_of(rings, early):
    column = [8 * z for z in range(rings)]
    if len(early) == 3:
        first, sent = [[0, 2, 4, 6], column[1:]], {k: column[1:] for k in early}
    else:
        first = [column] + [[2 * k] for k in early]
        sent = {k: column[1:] if k in early else column for k in (1, 2, 3)}
    chips = first + [[d ^ (2 * k) for d in sent[k]] for k in (1, 2, 3)]
    return chips + [[d ^ 1 for d in piece] for piece in chips]


def pack_blocks(*refs):
    parts, out_ref = refs[:-1], refs[-1]
    at = 0
    for part in parts:
        out_ref[at : at + part.shape[0], :] = part[...]
        at += part.shape[0]


def packed(parts):
    rows = sum(part.shape[0] for part in parts)
    return pl.pallas_call(
        pack_blocks,
        out_shape=shape(rows, parts[0].shape[1]),
        in_specs=[VMEM] * len(parts),
        out_specs=VMEM,
        compiler_params=params(2),
        cost_estimate=cost(0.5),
    )(*parts)


def gather(block, n, early):
    def swap(x, m):
        return lax.ppermute(x, "blk", [(i, i ^ m) for i in range(n)])

    far = [swap(block, 8 * z) for z in range(1, n // 8)]
    near = [swap(block, 2 * k) for k in early]
    if len(early) == 3:
        rest = packed(far)
        chips = [packed([block] + near), rest]
        sent = {k: rest for k in early}
    else:
        full = packed([block] + far)
        rest = packed(far) if early else None
        chips = [full] + near
        sent = {k: rest if k in early else full for k in (1, 2, 3)}
    chips += [swap(sent[k], 2 * k) for k in (1, 2, 3)]
    return chips + [swap(x, 1) for x in chips]


def assemble(me, pieces, rings, early, place):
    for piece, distances in zip(pieces, layout_of(rings, early)):
        for slot, distance in enumerate(distances):
            place(piece, slot, jnp.bitwise_xor(me, distance))


def first_product(rings, rows, me_ref, kernel_ref, diag_ref, *refs):
    pieces, (y_ref, ky_ref) = refs[:-2], refs[-2:]
    width = y_ref.shape[1] // 2

    def place(piece, slot, device):
        base = slot * 2 * rows
        at = pl.ds(pl.multiple_of(device * rows, rows), rows)
        y_ref[at, :width] = piece[base : base + rows, :]
        y_ref[at, width:] = piece[base + rows : base + 2 * rows, :]

    assemble(me_ref[0], pieces, rings, EARLY[0], place)
    result = mm3(kernel_ref[...], y_ref[...])
    ky_ref[:rows, :] = result[:, :width]
    ky_ref[rows : 2 * rows, :] = result[:, width:]
    ky_ref[2 * rows :, :] = jnp.zeros((8, width), F32)
    ky_ref[2 * rows : 2 * rows + 1, :rows] = diag_ref[...]


def metric_kernel(y_ref, out_ref):
    total, double = y_ref.shape
    width = double // 2

    def add(at, acc):
        top, rest = halves(y_ref[at, :])
        product = lax.dot_general(
            top,
            jnp.concatenate([top, rest], 1),
            (((0,), (0,)), ((), ())),
            preferred_element_type=F32,
        )
        return acc + product

    sums = sweep(total, add, jnp.zeros((double, 2 * double), F32))
    metric = sums[:, :double] + (sums[:, double:] + sums[:, double:].T)
    upper = inverse_factor(metric[:width, :width])
    cross = mm(upper, metric[:width, width:])
    lower = inverse_factor(metric[width:, width:] - mm(cross, cross, 0, 0))
    out_ref[:width, :width] = upper
    out_ref[:width, width:] = jnp.zeros((width, width), F32)
    out_ref[width:, :width] = -mm(lower, mm(cross, upper, 0, 0))
    out_ref[width:, width:] = lower


def divided(residual, diag, values):
    eye = lax.broadcasted_iota(jnp.int32, values.shape, 0) == lax.broadcasted_iota(
        jnp.int32, values.shape, 1
    )
    level = jnp.sum(jnp.where(eye, values, 0.0), axis=0, keepdims=True)
    return residual / jnp.maximum(jnp.abs(diag - level), 1.0)


def first_step(y_ref, ky_ref, factor_ref, diag_ref, y2_ref, kx_ref, small_ref, norm_ref):
    total, double = y_ref.shape
    width = double // 2
    rows = diag_ref.shape[0]

    def add(at, acc):
        return acc + mm3(y_ref[at, :], ky_ref[at, :], 0, 0)

    g = sweep(total, add, jnp.zeros((double, double), F32), 1024)
    factor = factor_ref[...]
    tie = g[:width, width:].T
    side = jnp.concatenate([g[:width, :width], tie], 0)
    whole = jnp.concatenate([g[:width, :], jnp.concatenate([tie, g[width:, width:]], 1)], 0)
    z = mm3(factor, side)
    small = inverse_factor(mm3(z, z, 0, 0))
    raw = mm3(factor, z, 0, 0)
    held = mm3(jnp.concatenate([raw, mm3(whole, raw)], 0), small, 1, 1)
    mixing = held[:double]
    values = mm3(mixing, held[double:], 0, 0)
    both = stacked(jnp.concatenate([mixing, mm3(mixing, values)], 1))
    mixing = stacked(mixing)
    small_ref[...] = values

    def update(at, acc):
        pair = with_stacked(y_ref[at, :], both)
        image = with_stacked(ky_ref[at, :], mixing)
        y2_ref[at, :width] = pair[:, :width]
        kx_ref[at, :] = image
        residual = image - pair[:, width:]
        y2_ref[at, width:] = residual
        return acc + jnp.sum(residual * residual, axis=0, keepdims=True)

    squares = sweep(total, update, jnp.zeros((1, width), F32))
    norm_ref[...] = jnp.sqrt(squares)
    for b in range(total // rows):
        at = pl.ds(b * rows, rows)
        y2_ref[at, width:] = divided(y2_ref[at, width:], diag_ref[:rows, b : b + 1], values)


def with_product(rings, rows, me_ref, kernel_ref, y_ref, factor_ref, *refs):
    pieces = refs[:-8]
    y2_ref, kx_ref, small_ref, norm_ref, kw_ref, ky_ref, table, diag_ref = refs[-8:]
    width = kx_ref.shape[1]
    step = 2 * rows + 8

    def place(piece, slot, device):
        base = slot * step
        at = pl.ds(pl.multiple_of(device * rows, rows), rows)
        ky_ref[at, :width] = piece[base : base + rows, :]
        ky_ref[at, width:] = piece[base + rows : base + 2 * rows, :]
        table[pl.ds(device, 1), :] = piece[base + 2 * rows : base + 2 * rows + 1, :]

    table[...] = jnp.zeros_like(table)
    assemble(me_ref[0], pieces, rings, EARLY[1], place)
    diag_ref[...] = table[...].T
    first_step(
        y_ref, ky_ref, factor_ref, diag_ref.at[:rows, :], y2_ref, kx_ref, small_ref, norm_ref
    )
    kw_ref[...] = mm3(kernel_ref[...], y2_ref[:, width:])


def second_gram(y2_ref, gram_ref):
    total, double = y2_ref.shape
    width = double // 2

    def add(at, acc):
        return acc + mm3(y2_ref[at, width:], y2_ref[at, :], 0, 0)

    gram_ref[...] = sweep(total, add, jnp.zeros((width, double), F32))


def second_factor(gram_ref, small_ref, tie_ref, factor_ref, known_ref, square_ref):
    width = small_ref.shape[0]
    tie = gram_ref[:, :width]
    values = small_ref[...]
    factor = inverse_factor(gram_ref[:, width:] - mm(tie, tie, 1, 1))
    tie_ref[...] = tie
    factor_ref[...] = factor
    known_ref[...] = mm(factor, mm(tie, values))
    square_ref[...] = mm(values, values, 0, 0)


def second_step(y2_ref, image_ref, known, first_ref, own_y2, own_image, own_diag, outs):
    ritz_ref, search_ref, norm_ref = outs
    total, double = y2_ref.shape
    width = double // 2

    def add(at, acc):
        return acc + mm3(image_ref[at, width:], y2_ref[at, :], 0, 0)

    g = sweep(total, add, jnp.zeros((width, double), F32))
    values, tie, factor, done, square = [ref[...] for ref in known]
    z = mm3(factor, g[:, :width]) - done
    small = inverse_factor(square + mm3(z, z, 0, 0))
    lower = mm3(factor, z, 0, 0)
    raw = jnp.concatenate([values - mm3(tie, lower, 0, 0), lower], 0)
    whole = jnp.concatenate([jnp.concatenate([values, g[:, :width].T], 1), g], 0)
    held = mm3(jnp.concatenate([raw, mm3(whole, raw)], 0), small, 1, 1)
    mixing = held[:double]
    values2 = mm3(mixing, held[double:], 0, 0)
    weights = stacked(jnp.concatenate([mixing, -mm3(mixing, values2)], 0))

    def update(at, acc):
        residual = with_stacked(jnp.concatenate([image_ref[at, :], y2_ref[at, :]], 1), weights)
        return acc + jnp.sum(residual * residual, axis=0, keepdims=True)

    squares = sweep(total, update, jnp.zeros((1, width), F32))
    norm_ref[:1, :] = first_ref[...]
    norm_ref[1:, :] = jnp.sqrt(squares)
    own = own_y2()
    ritz_ref[...] = mm3(own, mixing)
    residual = with_stacked(jnp.concatenate([own_image(), own], 1), weights)
    search_ref[...] = divided(residual, own_diag(), values2)


def last_step(rings, rows, me_ref, y2_ref, kx_ref, first_ref, diag_ref, *refs):
    known, pieces = refs[:5], refs[5:-4]
    ritz_ref, search_ref, norm_ref, image_ref = refs[-4:]
    width = kx_ref.shape[1]
    me = me_ref[0]

    def place(piece, slot, device):
        at = pl.ds(pl.multiple_of(device * rows, rows), rows)
        image_ref[at, width:] = piece[slot * rows : (slot + 1) * rows, :]

    assemble(me, pieces, rings, EARLY[2], place)
    image_ref[:, :width] = kx_ref[...]
    mine = pl.ds(pl.multiple_of(me * rows, rows), rows)
    second_step(
        y2_ref,
        image_ref,
        known,
        first_ref,
        lambda: y2_ref[mine, :],
        lambda: image_ref[mine, :],
        lambda: jnp.broadcast_to(diag_ref[...], (8, rows)).T[:, :1],
        (ritz_ref, search_ref, norm_ref),
    )


def general_last(y2_ref, image_ref, first_ref, own_y2, own_image, own_diag, *refs):
    known, outs = refs[:5], refs[5:]
    second_step(
        y2_ref,
        image_ref,
        known,
        first_ref,
        lambda: own_y2[...],
        lambda: own_image[...],
        lambda: own_diag[...],
        outs,
    )


def cost(us):
    return pl.CostEstimate(flops=int(us * 1e9), bytes_accessed=0, transcendentals=0)


def shape(*dims):
    return jax.ShapeDtypeStruct(dims, F32)


VMEM = pl.BlockSpec(memory_space=pltpu.VMEM)
SMEM = pl.BlockSpec(memory_space=pltpu.SMEM)


def metric_factor(y, mebibytes):
    double = y.shape[1]
    return pl.pallas_call(
        metric_kernel,
        out_shape=shape(double, double),
        in_specs=[VMEM],
        out_specs=VMEM,
        compiler_params=params(mebibytes),
        cost_estimate=cost(9),
        name="metric",
    )(y)


def second_metric(y2, values, mebibytes):
    width = y2.shape[1] // 2
    gram = pl.pallas_call(
        second_gram,
        out_shape=shape(width, 2 * width),
        in_specs=[VMEM],
        out_specs=VMEM,
        compiler_params=params(mebibytes),
        cost_estimate=cost(1),
        name="second_gram",
    )(y2)
    return pl.pallas_call(
        second_factor,
        out_shape=(shape(width, width),) * 4,
        in_specs=[VMEM] * 2,
        out_specs=(VMEM,) * 4,
        compiler_params=params(mebibytes),
        cost_estimate=cost(9),
        name="second_factor",
    )(gram, values)


def cubed(n, kernel, ritz, search, diag):
    rows, width = ritz.shape
    rings = n // 8
    total = n * rows
    lanes = max(n, 128)
    me = lax.axis_index("blk").astype(jnp.int32).reshape(1)
    along = diag.reshape(1, rows)
    own = lax.pad(ritz, 0.0, ((0, rows, 0), (0, 0, 0))) + lax.pad(search, 0.0, ((rows, 0, 0), (0, 0, 0)))
    sent = gather(own, n, EARLY[0])
    y, ky_own = pl.pallas_call(
        lambda *refs: first_product(rings, rows, *refs),
        out_shape=(shape(total, 2 * width), shape(2 * rows + 8, width)),
        in_specs=[SMEM, VMEM, VMEM] + [VMEM] * len(sent),
        out_specs=(VMEM, VMEM),
        compiler_params=params(16),
        name="first_product",
    )(me, kernel, along, *sent)
    images = gather(ky_own, n, EARLY[1])
    factor = metric_factor(y, 12)
    y2, kx, values, norm1, kw_own = pl.pallas_call(
        lambda *refs: with_product(rings, rows, *refs),
        out_shape=(
            shape(total, 2 * width),
            shape(total, width),
            shape(width, width),
            shape(1, width),
            shape(rows, width),
        ),
        in_specs=[SMEM] + [VMEM] * (3 + len(images)),
        out_specs=(VMEM,) * 5,
        scratch_shapes=[
            pltpu.VMEM((total, 2 * width), F32),
            pltpu.VMEM((lanes, width), F32),
            pltpu.VMEM((width, lanes), F32),
        ],
        compiler_params=params(24),
        name="first_step",
    )(me, kernel, y, factor, *images)
    images2 = gather(kw_own, n, EARLY[2])
    known = second_metric(y2, values, 12)
    return pl.pallas_call(
        lambda *refs: last_step(rings, rows, *refs),
        out_shape=(shape(rows, width), shape(rows, width), shape(ITERS, width)),
        in_specs=[SMEM] + [VMEM] * (9 + len(images2)),
        out_specs=(VMEM,) * 3,
        scratch_shapes=[pltpu.VMEM((total, 2 * width), F32)],
        compiler_params=params(24),
        name="last_step",
    )(me, y2, kx, norm1, along, values, *known, *images2)


def general(n, cols, kernel, ritz, search, diag):
    rows, width = ritz.shape
    axes = ("blk", "col")
    total = n * cols * rows
    q = lax.axis_index("col")

    def product(part):
        whole = lax.psum_scatter(mm(kernel, part), "col", scatter_dimension=0, tiled=True)
        return whole

    own = jnp.concatenate([ritz, search], 1)
    part = lax.all_gather(own, "blk", axis=0, tiled=True)
    y = lax.all_gather(own, axes, axis=0, tiled=True)
    ky = lax.all_gather(product(part), axes, axis=0, tiled=True)
    table = lax.all_gather(diag, axes, axis=0, tiled=True).reshape(n * cols, rows).T
    factor = metric_factor(y, 56)
    y2, kx, values, norm1 = pl.pallas_call(
        first_step,
        out_shape=(shape(total, 2 * width), shape(total, width), shape(width, width), shape(1, width)),
        in_specs=[VMEM] * 4,
        out_specs=(VMEM,) * 4,
        compiler_params=params(),
        name="first_step",
    )(y, ky, factor, table)
    held = y2[:, width:].reshape(n, cols, rows, width)
    part2 = lax.dynamic_index_in_dim(held, q, 1, keepdims=False).reshape(n * rows, width)
    kw = lax.all_gather(product(part2), axes, axis=0, tiled=True)
    known = second_metric(y2, values, 56)
    image = jnp.concatenate([kx, kw], 1)
    at = (lax.axis_index("blk") * cols + q) * rows
    return pl.pallas_call(
        general_last,
        out_shape=(shape(rows, width), shape(rows, width), shape(ITERS, width)),
        in_specs=[VMEM] * 11,
        out_specs=(VMEM,) * 3,
        compiler_params=params(),
        name="last_step",
    )(
        y2,
        image,
        norm1,
        lax.dynamic_slice_in_dim(y2, at, rows, 0),
        lax.dynamic_slice_in_dim(image, at, rows, 0),
        diag[:, None],
        values,
        *known,
    )


def solution(mesh):
    n, cols = mesh.shape["blk"], mesh.shape["col"]
    placed = (
        P("blk", "col", None),
        P(("blk", "col"), None),
        P(("blk", "col"), None),
        P(("blk", "col")),
    )

    cubes = cols == 1 and n >= 16 and n & (n - 1) == 0

    def per_device(kernel, ritz_block, search_block, precond_diag):
        rows = kernel[:, 0, :]
        if cubes:
            return cubed(n, rows, ritz_block, search_block, precond_diag)
        return general(n, cols, rows, ritz_block, search_block, precond_diag)

    return jax.shard_map(
        per_device,
        mesh=mesh,
        in_specs=placed,
        out_specs=(P(("blk", "col"), None), P(("blk", "col"), None), P()),
        check_vma=False,
    )
```

```python
import jax
import jax.numpy as jnp
from jax import lax
from jax.experimental import pallas as pl
from jax.experimental.pallas import tpu as pltpu
from jax.sharding import PartitionSpec as P


ITERS = 2
F32 = jnp.float32
BF16 = jnp.bfloat16
highest = lax.Precision.HIGHEST
CHUNK = 2048
EARLY = ((1, 2, 3), (1, 2, 3), (1, 2, 3))


def params(mebibytes=56):
    return pltpu.CompilerParams(vmem_limit_bytes=mebibytes << 20)


def mm(a, b, ca=1, cb=0):
    return lax.dot_general(
        a, b, (((ca,), (cb,)), ((), ())), precision=highest, preferred_element_type=F32
    )


def sweep(total, add, zero, chunk=CHUNK):
    chunk = min(chunk, total)
    if chunk == total:
        return add(pl.ds(0, total), zero)

    def part(i, acc):
        return add(pl.ds(pl.multiple_of(i * chunk, chunk), chunk), acc)

    return lax.fori_loop(0, total // chunk, part, zero)


def halves(x):
    top = x.astype(BF16)
    return top, (x - top.astype(F32)).astype(BF16)


def stacked(b, cb=0):
    b1, b2 = halves(b)
    return jnp.concatenate([b1, b2, b1], cb)


def mm3(a, b, ca=1, cb=0):
    return with_stacked(a, stacked(b, cb), ca, cb)


def with_stacked(a, b3, ca=1, cb=0):
    a1, a2 = halves(a)
    return lax.dot_general(
        jnp.concatenate([a1, a1, a2], ca),
        b3,
        (((ca,), (cb,)), ((), ())),
        preferred_element_type=F32,
    )


def pair_sum(terms):
    terms = list(terms)
    while len(terms) > 1:
        terms = [sum(terms[i + 1 : i + 2], terms[i]) for i in range(0, len(terms), 2)]
    return terms[0]


def total_of(xs, ys):
    return pair_sum(x * y for x, y in zip(xs, ys))


def solved(entry, columns, leaf):
    size = len(columns[0])
    if size == 2:
        x, y, z = entry(0, 0), entry(0, 1), entry(1, 1)
        scale = 1.0 / (x * z - y * y)
        q00, q01, q11 = z * scale, -(y * scale), x * scale
        leaf(x, y, z, columns[-1])
        return [[q00 * c[0] + q01 * c[1], q01 * c[0] + q11 * c[1]] for c in columns]
    h = size // 2
    side = [[entry(i, h + j) for i in range(h)] for j in range(h)]
    done = solved(entry, side + [c[:h] for c in columns], leaf)
    ties, upper = done[:h], done[h:]
    rest = {
        (i, j): entry(h + i, h + j) - total_of(side[i], ties[j])
        for j in range(h)
        for i in range(j + 1)
    }
    lower = solved(
        lambda i, j: rest[i, j],
        [[c[h + j] - total_of(ties[j], c[:h]) for j in range(h)] for c in columns],
        leaf,
    )
    return [
        [u[i] - total_of([ties[j][i] for j in range(h)], g) for i in range(h)] + g
        for u, g in zip(upper, lower)
    ]


def inverse_factor(matrix, panel=128):
    n, step = matrix.shape[0], 8
    lane = lax.broadcasted_iota(jnp.int32, (8, n), 1)
    sub = lax.broadcasted_iota(jnp.int32, (8, n), 0)
    a = [matrix[8 * v : 8 * v + 8, :] for v in range(n // 8)]
    zero = a[0] * 0.0

    def along(x, j):
        return jnp.broadcast_to(x[:, j : j + 1], (8, n))

    def down(x, i):
        return jnp.broadcast_to(x[i : i + 1, :], (8, n))

    rows = []
    for first in range(0, n, panel):
        last = (first + panel) // 8
        multipliers = []
        for k in range(first, first + panel, step):
            r = k // 8
            own = [along(a[r], k + j) + zero for j in range(step)]
            pivot = {(i, j): down(own[j], i) for j in range(step) for i in range(j + 1)}
            inside = (lane >= k) & (lane < k + step)
            base = jnp.where(inside, jnp.where(lane - k == sub, 1.0, 0.0), a[r])
            finished = []

            def leaf(x, y, z, e):
                scale = lax.rsqrt(x)
                ratio = y * (scale * scale)
                finished.append(e[0] * scale)
                finished.append((e[1] - ratio * e[0]) * lax.rsqrt(z - y * ratio))

            g = solved(lambda i, j: pivot[i, j], [[down(base, i) for i in range(step)]], leaf)[0]
            row, held = finished[0], g[0]
            for i in range(1, step):
                row = jnp.where(sub == i, finished[i], row)
                held = jnp.where(sub == i, g[i], held)
            rows.append(jnp.where(lane <= sub + k, row, 0.0))
            multipliers.append(
                jnp.where((lane >= k + step) & (lane < first + panel), 0.0, held)
            )
            for v in range(r + 1, last):
                other = [along(a[v], k + j) for j in range(step)]
                a[v] = jnp.where(inside, 0.0, a[v]) - total_of(other, g)
        if last < n // 8:
            change = mm(
                jnp.concatenate(a[first // 8 : last], 0), jnp.concatenate(multipliers, 0), 0, 0
            )
            inside = (lane >= first) & (lane < first + panel)
            for v in range(last, n // 8):
                a[v] = jnp.where(inside, 0.0, a[v]) - change[8 * v : 8 * v + 8]
    return jnp.concatenate(rows, 0)


def layout_of(rings, early):
    column = [8 * z for z in range(rings)]
    if len(early) == 3:
        first, sent = [[0, 2, 4, 6], column[1:]], {k: column[1:] for k in early}
    else:
        first = [column] + [[2 * k] for k in early]
        sent = {k: column[1:] if k in early else column for k in (1, 2, 3)}
    chips = first + [[d ^ (2 * k) for d in sent[k]] for k in (1, 2, 3)]
    return chips + [[d ^ 1 for d in piece] for piece in chips]


def pack_blocks(*refs):
    parts, out_ref = refs[:-1], refs[-1]
    at = 0
    for part in parts:
        out_ref[at : at + part.shape[0], :] = part[...]
        at += part.shape[0]


def packed(parts):
    rows = sum(part.shape[0] for part in parts)
    return pl.pallas_call(
        pack_blocks,
        out_shape=shape(rows, parts[0].shape[1]),
        in_specs=[VMEM] * len(parts),
        out_specs=VMEM,
        compiler_params=params(2),
        cost_estimate=cost(0.5),
    )(*parts)


def gather(block, n, early):
    def swap(x, m):
        return lax.ppermute(x, "blk", [(i, i ^ m) for i in range(n)])

    far = [swap(block, 8 * z) for z in range(1, n // 8)]
    near = [swap(block, 2 * k) for k in early]
    if len(early) == 3:
        rest = packed(far)
        chips = [packed([block] + near), rest]
        sent = {k: rest for k in early}
    else:
        full = packed([block] + far)
        rest = packed(far) if early else None
        chips = [full] + near
        sent = {k: rest if k in early else full for k in (1, 2, 3)}
    chips += [swap(sent[k], 2 * k) for k in (1, 2, 3)]
    return chips + [swap(x, 1) for x in chips]


def assemble(me, pieces, rings, early, place):
    for piece, distances in zip(pieces, layout_of(rings, early)):
        for slot, distance in enumerate(distances):
            place(piece, slot, jnp.bitwise_xor(me, distance))


def first_product(rings, rows, me_ref, kernel_ref, diag_ref, *refs):
    pieces, (y_ref, ky_ref) = refs[:-2], refs[-2:]
    width = y_ref.shape[1] // 2

    def place(piece, slot, device):
        base = slot * 2 * rows
        at = pl.ds(pl.multiple_of(device * rows, rows), rows)
        y_ref[at, :width] = piece[base : base + rows, :]
        y_ref[at, width:] = piece[base + rows : base + 2 * rows, :]

    assemble(me_ref[0], pieces, rings, EARLY[0], place)
    result = mm3(kernel_ref[...], y_ref[...])
    ky_ref[:rows, :] = result[:, :width]
    ky_ref[rows : 2 * rows, :] = result[:, width:]
    ky_ref[2 * rows :, :] = jnp.zeros((8, width), F32)
    ky_ref[2 * rows : 2 * rows + 1, :rows] = diag_ref[...]


def metric_kernel(y_ref, out_ref):
    total, double = y_ref.shape
    width = double // 2

    def add(at, acc):
        top, rest = halves(y_ref[at, :])
        product = lax.dot_general(
            top,
            jnp.concatenate([top, rest], 1),
            (((0,), (0,)), ((), ())),
            preferred_element_type=F32,
        )
        return acc + product

    sums = sweep(total, add, jnp.zeros((double, 2 * double), F32))
    metric = sums[:, :double] + (sums[:, double:] + sums[:, double:].T)
    upper = inverse_factor(metric[:width, :width])
    cross = mm(upper, metric[:width, width:])
    lower = inverse_factor(metric[width:, width:] - mm(cross, cross, 0, 0))
    out_ref[:width, :width] = upper
    out_ref[:width, width:] = jnp.zeros((width, width), F32)
    out_ref[width:, :width] = -mm(lower, mm(cross, upper, 0, 0))
    out_ref[width:, width:] = lower


def divided(residual, diag, values):
    eye = lax.broadcasted_iota(jnp.int32, values.shape, 0) == lax.broadcasted_iota(
        jnp.int32, values.shape, 1
    )
    level = jnp.sum(jnp.where(eye, values, 0.0), axis=0, keepdims=True)
    return residual / jnp.maximum(jnp.abs(diag - level), 1.0)


def first_step(y_ref, ky_ref, factor_ref, diag_ref, y2_ref, kx_ref, small_ref, norm_ref):
    total, double = y_ref.shape
    width = double // 2
    rows = diag_ref.shape[0]

    def add(at, acc):
        return acc + mm3(y_ref[at, :], ky_ref[at, :], 0, 0)

    g = sweep(total, add, jnp.zeros((double, double), F32), 1024)
    factor = factor_ref[...]
    tie = g[:width, width:].T
    side = jnp.concatenate([g[:width, :width], tie], 0)
    whole = jnp.concatenate([g[:width, :], jnp.concatenate([tie, g[width:, width:]], 1)], 0)
    z = mm3(factor, side)
    small = inverse_factor(mm3(z, z, 0, 0))
    raw = mm3(factor, z, 0, 0)
    held = mm3(jnp.concatenate([raw, mm3(whole, raw)], 0), small, 1, 1)
    mixing = held[:double]
    values = mm3(mixing, held[double:], 0, 0)
    both = stacked(jnp.concatenate([mixing, mm3(mixing, values)], 1))
    mixing = stacked(mixing)
    small_ref[...] = values

    def update(at, acc):
        pair = with_stacked(y_ref[at, :], both)
        image = with_stacked(ky_ref[at, :], mixing)
        y2_ref[at, :width] = pair[:, :width]
        kx_ref[at, :] = image
        residual = image - pair[:, width:]
        y2_ref[at, width:] = residual
        return acc + jnp.sum(residual * residual, axis=0, keepdims=True)

    squares = sweep(total, update, jnp.zeros((1, width), F32))
    norm_ref[...] = jnp.sqrt(squares)
    for b in range(total // rows):
        at = pl.ds(b * rows, rows)
        y2_ref[at, width:] = divided(y2_ref[at, width:], diag_ref[:rows, b : b + 1], values)


def with_product(rings, rows, me_ref, kernel_ref, y_ref, factor_ref, *refs):
    pieces = refs[:-8]
    y2_ref, kx_ref, small_ref, norm_ref, kw_ref, ky_ref, table, diag_ref = refs[-8:]
    width = kx_ref.shape[1]
    step = 2 * rows + 8

    def place(piece, slot, device):
        base = slot * step
        at = pl.ds(pl.multiple_of(device * rows, rows), rows)
        ky_ref[at, :width] = piece[base : base + rows, :]
        ky_ref[at, width:] = piece[base + rows : base + 2 * rows, :]
        table[pl.ds(device, 1), :] = piece[base + 2 * rows : base + 2 * rows + 1, :]

    table[...] = jnp.zeros_like(table)
    assemble(me_ref[0], pieces, rings, EARLY[1], place)
    diag_ref[...] = table[...].T
    first_step(
        y_ref, ky_ref, factor_ref, diag_ref.at[:rows, :], y2_ref, kx_ref, small_ref, norm_ref
    )
    kw_ref[...] = mm3(kernel_ref[...], y2_ref[:, width:])


def second_gram(y2_ref, gram_ref):
    total, double = y2_ref.shape
    width = double // 2

    def add(at, acc):
        return acc + mm3(y2_ref[at, width:], y2_ref[at, :], 0, 0)

    gram_ref[...] = sweep(total, add, jnp.zeros((width, double), F32))


def second_factor(gram_ref, small_ref, tie_ref, factor_ref, known_ref, square_ref):
    width = small_ref.shape[0]
    tie = gram_ref[:, :width]
    values = small_ref[...]
    factor = inverse_factor(gram_ref[:, width:] - mm(tie, tie, 1, 1))
    tie_ref[...] = tie
    factor_ref[...] = factor
    known_ref[...] = mm(factor, mm(tie, values))
    square_ref[...] = mm(values, values, 0, 0)


def second_step(y2_ref, image_ref, known, first_ref, own_y2, own_image, own_diag, outs):
    ritz_ref, search_ref, norm_ref = outs
    total, double = y2_ref.shape
    width = double // 2

    def add(at, acc):
        return acc + mm3(image_ref[at, width:], y2_ref[at, :], 0, 0)

    g = sweep(total, add, jnp.zeros((width, double), F32))
    values, tie, factor, done, square = [ref[...] for ref in known]
    z = mm3(factor, g[:, :width]) - done
    small = inverse_factor(square + mm3(z, z, 0, 0))
    lower = mm3(factor, z, 0, 0)
    raw = jnp.concatenate([values - mm3(tie, lower, 0, 0), lower], 0)
    whole = jnp.concatenate([jnp.concatenate([values, g[:, :width].T], 1), g], 0)
    held = mm3(jnp.concatenate([raw, mm3(whole, raw)], 0), small, 1, 1)
    mixing = held[:double]
    values2 = mm3(mixing, held[double:], 0, 0)
    turned = stacked(mm3(mixing, values2))
    weights = stacked(mixing)

    def update(at, acc):
        residual = with_stacked(image_ref[at, :], weights) - with_stacked(y2_ref[at, :], turned)
        return acc + jnp.sum(residual * residual, axis=0, keepdims=True)

    squares = sweep(total, update, jnp.zeros((1, width), F32))
    norm_ref[:1, :] = first_ref[...]
    norm_ref[1:, :] = jnp.sqrt(squares)
    own = own_y2()
    ritz_ref[...] = mm3(own, mixing)
    residual = with_stacked(own_image(), weights) - with_stacked(own, turned)
    search_ref[...] = divided(residual, own_diag(), values2)


def last_step(rings, rows, me_ref, y2_ref, kx_ref, first_ref, diag_ref, *refs):
    known, pieces = refs[:5], refs[5:-4]
    ritz_ref, search_ref, norm_ref, image_ref = refs[-4:]
    width = kx_ref.shape[1]
    me = me_ref[0]

    def place(piece, slot, device):
        at = pl.ds(pl.multiple_of(device * rows, rows), rows)
        image_ref[at, width:] = piece[slot * rows : (slot + 1) * rows, :]

    assemble(me, pieces, rings, EARLY[2], place)
    image_ref[:, :width] = kx_ref[...]
    mine = pl.ds(pl.multiple_of(me * rows, rows), rows)
    second_step(
        y2_ref,
        image_ref,
        known,
        first_ref,
        lambda: y2_ref[mine, :],
        lambda: image_ref[mine, :],
        lambda: jnp.broadcast_to(diag_ref[...], (8, rows)).T[:, :1],
        (ritz_ref, search_ref, norm_ref),
    )


def general_last(y2_ref, image_ref, first_ref, own_y2, own_image, own_diag, *refs):
    known, outs = refs[:5], refs[5:]
    second_step(
        y2_ref,
        image_ref,
        known,
        first_ref,
        lambda: own_y2[...],
        lambda: own_image[...],
        lambda: own_diag[...],
        outs,
    )


def cost(us):
    return pl.CostEstimate(flops=int(us * 1e9), bytes_accessed=0, transcendentals=0)


def shape(*dims):
    return jax.ShapeDtypeStruct(dims, F32)


VMEM = pl.BlockSpec(memory_space=pltpu.VMEM)
SMEM = pl.BlockSpec(memory_space=pltpu.SMEM)


def metric_factor(y, mebibytes):
    double = y.shape[1]
    return pl.pallas_call(
        metric_kernel,
        out_shape=shape(double, double),
        in_specs=[VMEM],
        out_specs=VMEM,
        compiler_params=params(mebibytes),
        cost_estimate=cost(9),
        name="metric",
    )(y)


def second_metric(y2, values, mebibytes):
    width = y2.shape[1] // 2
    gram = pl.pallas_call(
        second_gram,
        out_shape=shape(width, 2 * width),
        in_specs=[VMEM],
        out_specs=VMEM,
        compiler_params=params(mebibytes),
        cost_estimate=cost(1),
        name="second_gram",
    )(y2)
    return pl.pallas_call(
        second_factor,
        out_shape=(shape(width, width),) * 4,
        in_specs=[VMEM] * 2,
        out_specs=(VMEM,) * 4,
        compiler_params=params(mebibytes),
        cost_estimate=cost(9),
        name="second_factor",
    )(gram, values)


def cubed(n, kernel, ritz, search, diag):
    rows, width = ritz.shape
    rings = n // 8
    total = n * rows
    lanes = max(n, 128)
    me = lax.axis_index("blk").astype(jnp.int32).reshape(1)
    along = diag.reshape(1, rows)
    own = lax.pad(ritz, 0.0, ((0, rows, 0), (0, 0, 0))) + lax.pad(search, 0.0, ((rows, 0, 0), (0, 0, 0)))
    sent = gather(own, n, EARLY[0])
    y, ky_own = pl.pallas_call(
        lambda *refs: first_product(rings, rows, *refs),
        out_shape=(shape(total, 2 * width), shape(2 * rows + 8, width)),
        in_specs=[SMEM, VMEM, VMEM] + [VMEM] * len(sent),
        out_specs=(VMEM, VMEM),
        compiler_params=params(16),
        name="first_product",
    )(me, kernel, along, *sent)
    images = gather(ky_own, n, EARLY[1])
    factor = metric_factor(y, 12)
    y2, kx, values, norm1, kw_own = pl.pallas_call(
        lambda *refs: with_product(rings, rows, *refs),
        out_shape=(
            shape(total, 2 * width),
            shape(total, width),
            shape(width, width),
            shape(1, width),
            shape(rows, width),
        ),
        in_specs=[SMEM] + [VMEM] * (3 + len(images)),
        out_specs=(VMEM,) * 5,
        scratch_shapes=[
            pltpu.VMEM((total, 2 * width), F32),
            pltpu.VMEM((lanes, width), F32),
            pltpu.VMEM((width, lanes), F32),
        ],
        compiler_params=params(24),
        name="first_step",
    )(me, kernel, y, factor, *images)
    images2 = gather(kw_own, n, EARLY[2])
    known = second_metric(y2, values, 12)
    return pl.pallas_call(
        lambda *refs: last_step(rings, rows, *refs),
        out_shape=(shape(rows, width), shape(rows, width), shape(ITERS, width)),
        in_specs=[SMEM] + [VMEM] * (9 + len(images2)),
        out_specs=(VMEM,) * 3,
        scratch_shapes=[pltpu.VMEM((total, 2 * width), F32)],
        compiler_params=params(24),
        name="last_step",
    )(me, y2, kx, norm1, along, values, *known, *images2)


def general(n, cols, kernel, ritz, search, diag):
    rows, width = ritz.shape
    axes = ("blk", "col")
    total = n * cols * rows
    q = lax.axis_index("col")

    def product(part):
        whole = lax.psum_scatter(mm(kernel, part), "col", scatter_dimension=0, tiled=True)
        return whole

    own = jnp.concatenate([ritz, search], 1)
    part = lax.all_gather(own, "blk", axis=0, tiled=True)
    y = lax.all_gather(own, axes, axis=0, tiled=True)
    ky = lax.all_gather(product(part), axes, axis=0, tiled=True)
    table = lax.all_gather(diag, axes, axis=0, tiled=True).reshape(n * cols, rows).T
    factor = metric_factor(y, 56)
    y2, kx, values, norm1 = pl.pallas_call(
        first_step,
        out_shape=(shape(total, 2 * width), shape(total, width), shape(width, width), shape(1, width)),
        in_specs=[VMEM] * 4,
        out_specs=(VMEM,) * 4,
        compiler_params=params(),
        name="first_step",
    )(y, ky, factor, table)
    held = y2[:, width:].reshape(n, cols, rows, width)
    part2 = lax.dynamic_index_in_dim(held, q, 1, keepdims=False).reshape(n * rows, width)
    kw = lax.all_gather(product(part2), axes, axis=0, tiled=True)
    known = second_metric(y2, values, 56)
    image = jnp.concatenate([kx, kw], 1)
    at = (lax.axis_index("blk") * cols + q) * rows
    return pl.pallas_call(
        general_last,
        out_shape=(shape(rows, width), shape(rows, width), shape(ITERS, width)),
        in_specs=[VMEM] * 11,
        out_specs=(VMEM,) * 3,
        compiler_params=params(),
        name="last_step",
    )(
        y2,
        image,
        norm1,
        lax.dynamic_slice_in_dim(y2, at, rows, 0),
        lax.dynamic_slice_in_dim(image, at, rows, 0),
        diag[:, None],
        values,
        *known,
    )


def solution(mesh):
    n, cols = mesh.shape["blk"], mesh.shape["col"]
    placed = (
        P("blk", "col", None),
        P(("blk", "col"), None),
        P(("blk", "col"), None),
        P(("blk", "col")),
    )

    cubes = cols == 1 and n >= 16 and n & (n - 1) == 0

    def per_device(kernel, ritz_block, search_block, precond_diag):
        rows = kernel[:, 0, :]
        if cubes:
            return cubed(n, rows, ritz_block, search_block, precond_diag)
        return general(n, cols, rows, ritz_block, search_block, precond_diag)

    return jax.shard_map(
        per_device,
        mesh=mesh,
        in_specs=placed,
        out_specs=(P(("blk", "col"), None), P(("blk", "col"), None), P()),
        check_vma=False,
    )
```
